32 devices in a mesh: shot: 16 (over z, y, core), rcv: 2 (over x).
Axes of the slice: x: 2, y: 2, z: 4, core: 2. Of those that a mesh axis runs over, the one named last changes fastest.
Arguments:
- record: bfloat16 [768, 131072], P('rcv', 'shot'), may hold values from -6 to 6
- shot_fire_samples: int32 [512], P('shot'), may hold values from 0 to 131071, as said below
Outputs:
- psf_gram: float32 [2, 4, 768, 768], P(None, None, 'rcv', 'shot')
The draws below stay inside these ranges and needn't reach their ends.
Inputs may be any that keep to these rules, and one draw needn't show every extreme that they name: `shot_fire_samples`: shot s fires at a sample from s * 256 to s * 256 + 255.
All inputs are finite; a program needn't handle non-finite values.
Results may differ from the reference program's by a relative error of at most 0.0025.
Values may be sent and summed in bfloat16 or wider, within the bound.
A program may use at most 64 MiB of HBM per device.

```python
import math
import jax
import jax.numpy as jnp
from jax import lax

R = 768
WIN = 2048
F = 4
SPACING = 256
SHOTS_PER_UNIT = 32
SHOTS = 512
NT = 131072
N_SHOT = 16


def draw_shot_fire_samples(key, part):
    jitter = jax.random.randint(jax.random.fold_in(key, 7), (SHOTS,), 0, SPACING)
    return (jnp.arange(SHOTS, dtype=jnp.int32) * SPACING + jitter).astype(jnp.int32)


def shard_levels(key, shape, split, least, top_value):
    level, own = 1.0, jax.random.fold_in(key, 6)
    for dim, blocks in split:
        steps = jnp.exp(jax.random.uniform(jax.random.fold_in(own, dim), (blocks,), jnp.float32, least / len(split), top_value / len(split)))
        level = level * jnp.repeat(steps, shape[dim] // blocks).reshape([-1 if axis == dim else 1 for axis in range(len(shape))])
    return level


def normal_values(stream_key, shape, deviation, limit, split=(), kind=jnp.bfloat16):
    drawn = jax.random.normal(stream_key, shape, jnp.float32) * deviation
    if len(split) > 0:
        drawn = shard_levels(stream_key, shape, split, -0.22, 0.18) * drawn
    return jnp.clip(drawn, min=-limit, max=limit).astype(kind)


def setup_inputs(seed: int = 0) -> dict:
    arg_keys = jax.random.split(jax.random.key(seed), 3)
    record = normal_values(arg_keys[0], (R, NT), 1.0, 6.0, ((0, 2), (1, 16)))
    shot_fire_samples = draw_shot_fire_samples(jax.random.fold_in(arg_keys[2], 71), 0)
    return {"record": record, "shot_fire_samples": shot_fire_samples}


freq_bins = (24, 40, 56, 80)

def dft_table(window_len):
    lag_index = jnp.arange(window_len, dtype=jnp.int32)
    bin_list = jnp.array(freq_bins, dtype=jnp.int32)
    turn_count = lag_index[:, None] * bin_list[None, :] % window_len
    phase_angle = 2.0 * math.pi / window_len * turn_count.astype(jnp.float32)
    dft_rows = jnp.concatenate([jnp.cos(phase_angle), -jnp.sin(phase_angle)], axis=1) / math.sqrt(window_len)
    return dft_rows.astype(jnp.bfloat16)

def gram_terms(left, right):
    nfreq = len(freq_bins)
    left_re = left[:, :nfreq, :].astype(jnp.float32)
    left_im = left[:, nfreq:, :].astype(jnp.float32)
    right_re = right[:, :nfreq, :].astype(jnp.float32)
    right_im = right[:, nfreq:, :].astype(jnp.float32)
    gram_real = jnp.einsum('sfr,sfq->frq', left_re, right_re) + jnp.einsum('sfr,sfq->frq', left_im, right_im)
    gram_imag = jnp.einsum('sfr,sfq->frq', left_re, right_im) - jnp.einsum('sfr,sfq->frq', left_im, right_re)
    return jnp.stack([gram_real, gram_imag], axis=0)

def reference(record, shot_fire_samples):
    padded = jnp.concatenate([record, jnp.zeros((R, WIN), record.dtype)], axis=1)
    dft_rows = dft_table(WIN)

    def spectra_block(block_times):

        def cut_window(begin_at):
            return lax.dynamic_slice_in_dim(padded, begin_at.astype(jnp.int32), WIN, 1)
        windows = jax.vmap(cut_window)(block_times)
        flat = jnp.dot(windows.reshape(-1, WIN), dft_rows, preferred_element_type=jnp.float32)
        return flat.reshape(SHOTS_PER_UNIT, R, 2 * F).transpose(0, 2, 1).astype(jnp.bfloat16)
    trace_spectra = lax.map(spectra_block, shot_fire_samples.reshape(N_SHOT, SHOTS_PER_UNIT))
    trace_spectra = trace_spectra.reshape(SHOTS, 2 * F, R)
    return gram_terms(trace_spectra, trace_spectra) / SHOTS
```

```python
import functools
import math

import jax
import jax.numpy as jnp
from jax import lax
from jax.experimental import pallas as pl
from jax.experimental.pallas import tpu as pltpu
from jax.sharding import PartitionSpec as P

WIN = 2048
SPACING = 256


freq_bins = (24, 40, 56, 80)


def shifted(block, axis, distance):
    devices = range(lax.axis_size(axis))
    route = [(i - distance, i) for i in devices if i - distance in devices]
    return lax.ppermute(block, axis, route)


def dft_table(window_len):
    lag_index = jnp.arange(window_len, dtype=jnp.int32)
    bin_list = jnp.array(freq_bins, dtype=jnp.int32)
    turn_count = lag_index[:, None] * bin_list[None, :] % window_len
    phase_angle = 2.0 * math.pi / window_len * turn_count.astype(jnp.float32)
    dft_rows = jnp.concatenate([jnp.cos(phase_angle), -jnp.sin(phase_angle)], axis=1) / math.sqrt(
        window_len
    )
    return dft_rows.astype(jnp.bfloat16)


def shifted_tables(jitter, span):
    lag_index = jnp.arange(span, dtype=jnp.int32)[None, :] - jitter[:, None]
    inside = (lag_index >= 0) & (lag_index < WIN)
    clipped = jnp.clip(lag_index, 0, WIN - 1)
    bin_list = jnp.array(freq_bins, dtype=jnp.int32)
    turn_count = clipped[:, None, :] * bin_list[None, :, None] % WIN
    phase_angle = 2.0 * math.pi / WIN * turn_count.astype(jnp.float32)
    table = jnp.concatenate([jnp.cos(phase_angle), -jnp.sin(phase_angle)], axis=1) / math.sqrt(WIN)
    table = jnp.where(inside[:, None, :], table, 0.0)
    return table.astype(jnp.bfloat16)


def local_spectra(extended, sample_offsets, dft_rows):
    count_of_shots = sample_offsets.shape[0]
    reach_blocks = WIN // SPACING + 1
    jitter = sample_offsets - jnp.arange(count_of_shots, dtype=jnp.int32) * SPACING
    tables = shifted_tables(jitter, reach_blocks * SPACING)
    tables = tables.reshape(count_of_shots, dft_rows.shape[1], reach_blocks, SPACING)
    blocks = extended.reshape(extended.shape[0], extended.shape[1] // SPACING, SPACING)
    total = jnp.zeros((count_of_shots, dft_rows.shape[1], extended.shape[0]), jnp.float32)
    for offset in range(reach_blocks):
        record_part = blocks[:, offset : offset + count_of_shots, :]
        total = total + jnp.einsum(
            "rsu,scu->scr", record_part, tables[:, :, offset, :], preferred_element_type=jnp.float32
        )
    return total


def gram_terms(left, right):
    nfreq = len(freq_bins)
    left_re = left[:, :nfreq, :]
    left_im = left[:, nfreq:, :]
    right_re = right[:, :nfreq, :]
    right_im = right[:, nfreq:, :]
    gram_real = jnp.einsum("sfr,sfq->frq", left_re, right_re, preferred_element_type=jnp.float32)
    gram_real = gram_real + jnp.einsum(
        "sfr,sfq->frq", left_im, right_im, preferred_element_type=jnp.float32
    )
    gram_imag = jnp.einsum("sfr,sfq->frq", left_re, right_im, preferred_element_type=jnp.float32)
    gram_imag = gram_imag - jnp.einsum(
        "sfr,sfq->frq", left_im, right_re, preferred_element_type=jnp.float32
    )
    return jnp.stack([gram_real, gram_imag], axis=0)


def per_device(record, shot_fire_samples):
    trace_segment_length = record.shape[1]
    count_of_shots = shot_fire_samples.shape[0]
    dft_rows = dft_table(WIN)
    sample_offsets = shot_fire_samples - lax.axis_index("shot") * trace_segment_length
    head_rows = record[:, :WIN]
    rim_rows = shifted(head_rows, "shot", -1)
    extended = jnp.concatenate([record, rim_rows], axis=1)
    trace_spectra = local_spectra(extended, sample_offsets, dft_rows)
    trace_spectra = trace_spectra.astype(jnp.bfloat16)
    all_receivers = lax.all_gather(trace_spectra, "rcv", axis=2, tiled=True)
    total_shots = count_of_shots * lax.axis_size("shot")
    row_side = lax.all_gather(trace_spectra, "shot", axis=0, tiled=True)
    column_side = lax.all_to_all(all_receivers, "shot", split_axis=2, concat_axis=0, tiled=True)
    result = gram_terms(row_side, column_side)
    return result / total_shots


LANES = 128
HALF = 16
GROUP = 8
MESH = pl.DeviceIdType.MESH


def lane_fields(shape):
    lane = lax.broadcasted_iota(jnp.int32, shape, len(shape) - 1)
    return lane // 32 % 4, lane // 16 % 2, lane % 16


def rotated(lag):
    freq, part, _ = lane_fields((1, LANES))
    bins = jnp.full((1, LANES), freq_bins[0], jnp.int32)
    for f in range(1, len(freq_bins)):
        bins = jnp.where(freq == f, freq_bins[f], bins)
    turn = (lag & (SPACING - 1)) * bins + part * (WIN // 4)
    turn = ((turn + WIN // 2) & (WIN - 1)) - WIN // 2
    x = (math.pi / WIN) * turn.astype(jnp.float32)
    y = x * x
    series = 1.0 / math.factorial(13)
    for k in (11, 9, 7, 5, 3, 1):
        series = series * y + (-1.0) ** (k // 2) / math.factorial(k)
    half_sine = x * series
    return (1.0 - 2.0 * half_sine * half_sine) / math.sqrt(WIN)


def kernel(
    n, fire_hbm, rec_ref, out_ref,
    fire_ref, fire_sem, rec, joff, poff, table, tmask, rim_out, rim_in, gat, col, rmat, acc,
    rec_sem, jit_sem, rim_sem, ring_send, pair_send, chunk_recv, col_send, col_recv,
):
    me = lax.axis_index("shot")
    mj = lax.axis_index("rcv")
    rows = rec.shape[0]
    span = GROUP * SPACING
    chips = n // 2
    nz = chips // 2
    ncol = col.shape[2]
    shift, reach = SPACING.bit_length() - 1, WIN // SPACING
    core = me % 2
    chip = me // 2
    z, y = chip // 2, chip % 2
    pos = jnp.where(y == 0, z, chips - 1 - z)

    def device_at(position, which):
        q = (position + 2 * chips) % chips
        second = q >= nz
        zz = jnp.where(second, chips - 1 - q, q)
        yy = jnp.where(second, 1, 0)
        return (zz * 2 + yy) * 2 + which

    cw, ccw = device_at(pos + 1, core), device_at(pos - 1, core)
    pair = chip * 2 + (1 - core)
    prev, nxt = jnp.maximum(me - 1, 0), jnp.minimum(me + 1, n - 1)

    def load(g):
        part = pl.ds(g * span, span)
        return pltpu.make_async_copy(rec_ref.at[:, part], rec.at[:, part], rec_sem.at[g])

    fires = pltpu.make_async_copy(fire_hbm, fire_ref, fire_sem)
    fires.start()
    for g in (1, 2, 0, 3):
        load(g).start()

    barrier = pltpu.get_barrier_semaphore()
    has_prev, has_next = me > 0, me < n - 1

    def greet(other, column):
        pl.semaphore_signal(barrier, inc=1, device_id=(other, column), device_id_type=MESH)

    for other in (cw, ccw, pair):
        greet(other, mj)
    greet(me, 1 - mj)
    pl.when(has_prev)(lambda: greet(prev, mj))
    pl.when(has_next)(lambda: greet(nxt, mj))
    fires.wait()
    _, _, shot_lane = lane_fields((1, LANES))
    offs = []
    for h in range(2):
        row = jnp.zeros((1, LANES), jnp.int32)
        for s in range(HALF):
            row = jnp.where(shot_lane == s, fire_ref[h * HALF + s], row)
        offs.append(row - me * rec.shape[1])
    joff[...] = jnp.broadcast_to(offs[1], joff.shape)

    @pl.when(me == 0)
    def _():
        poff[...] = jnp.zeros_like(poff)

    jitter = pltpu.make_async_remote_copy(
        joff, poff, jit_sem.at[0], jit_sem.at[1], device_id=(nxt, mj), device_id_type=MESH
    )

    def fill_tables(kind, off_row):
        u = lax.broadcasted_iota(jnp.int32, (SPACING, LANES), 0)
        start = off_row & (SPACING - 1)
        value = rotated(u - start)
        table[kind, 0] = jnp.where(u >= start, value, 0.0).astype(jnp.bfloat16)
        table[kind, 1] = jnp.where(u < start, value, 0.0).astype(jnp.bfloat16)

    def group_dot(g, kinds):
        for slot, (kind, off_row) in enumerate(kinds):
            block_of = jnp.broadcast_to(off_row >> shift, (16, LANES))
            lanes = slice(slot * LANES, (slot + 1) * LANES)
            for b in range(GROUP):
                order = g * GROUP + b - block_of
                early = ((order >= 0) & (order < reach)).astype(jnp.float32).astype(jnp.bfloat16)
                late = ((order >= 1) & (order <= reach)).astype(jnp.float32).astype(jnp.bfloat16)
                block = (SPACING // 16, 16, LANES)
                mixed = table[kind, 0].reshape(block) * early + table[kind, 1].reshape(block) * late
                tmask[b * SPACING : (b + 1) * SPACING, lanes] = mixed.reshape(SPACING, LANES)
        return jnp.dot(
            rec[:, g * span : (g + 1) * span], tmask[:, : len(kinds) * LANES],
            preferred_element_type=jnp.float32,
        )

    def ring(src, h, d):
        return pltpu.make_async_remote_copy(
            gat.at[src, h], gat.at[src, h], ring_send, chunk_recv.at[src, h],
            device_id=(cw if d == 0 else ccw, mj), device_id_type=MESH,
        )

    def share(src, h):
        return pltpu.make_async_remote_copy(
            gat.at[src, h], gat.at[src, h], pair_send, chunk_recv.at[src, h],
            device_id=(pair, mj), device_id_type=MESH,
        )

    home = me * ncol // rows
    provider = home == mj
    first = pl.multiple_of(jnp.where(provider, me * ncol - home * rows, 0), 16)

    def col_far(src, h):
        return pltpu.make_async_remote_copy(
            gat.at[src, h, pl.ds(first, ncol), :], col.at[src, h], col_send,
            col_recv.at[src, h], device_id=(me, 1 - mj), device_id_type=MESH,
        )

    def col_near(src, h):
        return pltpu.make_async_copy(
            gat.at[src, h, pl.ds(first, ncol), :], col.at[src, h], col_recv.at[src, h]
        )

    def send_col(src, h):
        @pl.when(provider)
        def _():
            col_far(src, h).start()
            col_near(src, h).start()

    def send_own(h):
        ring(me, h, h).start()
        ring(me, h, 1 - h).start()
        share(me, h).start()
        send_col(me, h)

    def gram(src):
        for h in range(2):
            x = col[src, h].astype(jnp.float32)
            freq, part, _ = lane_fields(x.shape)
            swapped = jnp.where(part == 0, pltpu.roll(x, LANES - 16, 1), -pltpu.roll(x, 16, 1))
            for ri, value in enumerate((x, swapped)):
                for f in range(4):
                    rmat[pl.ds((ri * 4 + f) * ncol, ncol), h * LANES : (h + 1) * LANES] = jnp.where(
                        freq == f, value, 0.0
                    ).astype(jnp.bfloat16)
        left = jnp.concatenate([gat[src, 0], gat[src, 1]], axis=1)
        acc[...] += lax.dot_general(
            rmat[...], left, (((1,), (1,)), ((), ())), preferred_element_type=jnp.float32
        )

    fill_tables(0, offs[0])
    fill_tables(1, offs[1])
    acc[...] = jnp.zeros_like(acc)
    kinds = ((0, offs[0]), (1, offs[1]))
    load(1).wait()
    own = group_dot(1, kinds[:1])
    pl.semaphore_wait(barrier, 4 + has_prev.astype(jnp.int32) + has_next.astype(jnp.int32))
    pl.when(has_next)(jitter.start)
    load(2).wait()
    both = group_dot(2, kinds)
    load(0).wait()
    own = own + both[:, :LANES] + group_dot(0, kinds[:1])
    gat[me, 0] = own.astype(jnp.bfloat16)
    send_own(0)
    pl.when(has_prev)(jitter.wait_recv)
    offp = poff[0:1, :] - rec.shape[1]
    fill_tables(2, offp)
    foreign = group_dot(0, ((2, offp),))
    cut = rows // 2
    rim_out[...] = foreign[:cut] + pltpu.roll(foreign[cut:], LANES - 8, 1)
    rim = pltpu.make_async_remote_copy(
        rim_out, rim_in, rim_sem.at[0], rim_sem.at[1], device_id=(prev, mj), device_id_type=MESH
    )
    pl.when(has_prev)(rim.start)
    load(3).wait()
    second = both[:, LANES:] + group_dot(3, kinds[1:])
    pl.when(has_next)(rim.wait_recv)
    _, _, shot = lane_fields((cut, LANES))
    wanted = (shot >= 8) & (me < n - 1)
    upper = jnp.where(wanted, rim_in[...], 0.0)
    lower = jnp.where(wanted, pltpu.roll(rim_in[...], 8, 1), 0.0)
    gat[me, 1, :cut] = (second[:cut] + upper).astype(jnp.bfloat16)
    gat[me, 1, cut:] = (second[cut:] + lower).astype(jnp.bfloat16)
    send_own(1)

    half = chips // 2

    def hops(h, d):
        return half if h == d else half - 1

    def arrivals(t):
        found = []
        for h in range(2):
            for d in range(2):
                if 1 <= t <= hops(h, d):
                    found.append((h, d))
        return found

    def source(t, d, which):
        return device_at(pos - t if d == 0 else pos + t, which)

    def step_sources(t):
        if t == 0:
            return [0]
        return [0, 1] if t < half else [0]

    def gram_step(t):
        for which in (core, 1 - core):
            for d in step_sources(t):
                src = source(t, d, which)
                for h in range(2):
                    col_near(src, h).wait()
                gram(src)

    for t in range(half + 1):
        for h, d in arrivals(t):
            src = source(t, d, core)
            ring(src, h, d).wait_recv()
            if t < hops(h, d):
                ring(src, h, d).start()
            share(src, h).start()
            send_col(src, h)
        if t > 0:
            gram_step(t - 1)
        for d in step_sources(t):
            for h in range(2):
                src = source(t, d, 1 - core)
                share(src, h).wait_recv()
                send_col(src, h)
    gram_step(half)

    scale = 1.0 / (n * 2 * HALF)
    for g in range(8):
        out_ref[g // 4, g % 4] = acc[g * ncol : (g + 1) * ncol, :] * scale

    def drain(buffer, sem):
        pltpu.make_async_copy(buffer, buffer, sem).wait()

    pl.when(has_next)(jitter.wait_send)
    pl.when(has_prev)(rim.wait_send)
    drain(gat.at[pl.ds(0, chips - 1)], ring_send)
    drain(gat.at[pl.ds(0, chips)], pair_send)
    pl.when(provider)(lambda: drain(col, col_send))


def fused_device(n, ncol, record, shot_fire_samples):
    rows, length = record.shape
    shot_fire_samples = pltpu.with_memory_space_constraint(shot_fire_samples, pltpu.HBM)
    gram = pl.pallas_call(
        functools.partial(kernel, n),
        out_shape=jax.ShapeDtypeStruct((2, 4, ncol, rows), jnp.float32),
        in_specs=[
            pl.BlockSpec(memory_space=pltpu.HBM),
            pl.BlockSpec(memory_space=pltpu.HBM),
        ],
        out_specs=pl.BlockSpec(memory_space=pltpu.VMEM),
        scratch_shapes=[
            pltpu.SMEM(shot_fire_samples.shape, jnp.int32),
            pltpu.SemaphoreType.DMA,
            pltpu.VMEM((rows, length), jnp.bfloat16),
            pltpu.VMEM((8, LANES), jnp.int32),
            pltpu.VMEM((8, LANES), jnp.int32),
            pltpu.VMEM((3, 2, SPACING, LANES), jnp.bfloat16),
            pltpu.VMEM((GROUP * SPACING, 2 * LANES), jnp.bfloat16),
            pltpu.VMEM((rows // 2, LANES), jnp.float32),
            pltpu.VMEM((rows // 2, LANES), jnp.float32),
            pltpu.VMEM((n, 2, rows, LANES), jnp.bfloat16),
            pltpu.VMEM((n, 2, ncol, LANES), jnp.bfloat16),
            pltpu.VMEM((8 * ncol, 2 * LANES), jnp.bfloat16),
            pltpu.VMEM((8 * ncol, rows), jnp.float32),
            pltpu.SemaphoreType.DMA((length // (GROUP * SPACING),)),
            pltpu.SemaphoreType.DMA((2,)),
            pltpu.SemaphoreType.DMA((2,)),
            pltpu.SemaphoreType.DMA,
            pltpu.SemaphoreType.DMA,
            pltpu.SemaphoreType.DMA((n, 2)),
            pltpu.SemaphoreType.DMA,
            pltpu.SemaphoreType.DMA((n, 2)),
        ],
        compiler_params=pltpu.CompilerParams(
            collective_id=0, has_side_effects=True, vmem_limit_bytes=50 * 1024 * 1024
        ),
    )(shot_fire_samples, record)
    return gram.transpose(0, 1, 3, 2)


def whole_step(n, receivers, record, shot_fire_samples):
    rows, length = record.shape
    shots = shot_fire_samples.shape[0]
    ncol = receivers // n
    fits = (
        receivers == 2 * rows and ncol % 16 == 0 and rows % (2 * ncol) == 0
        and shots == 2 * HALF and length == shots * SPACING and n % 8 == 0
    )
    if fits:
        return fused_device(n, ncol, record, shot_fire_samples)
    return per_device(record, shot_fire_samples)


def solution(mesh):
    def step(record, shot_fire_samples):
        body = functools.partial(whole_step, mesh.shape["shot"], record.shape[0])
        return jax.shard_map(
            body,
            mesh=mesh,
            in_specs=(P("rcv", "shot"), P("shot")),
            out_specs=P(None, None, "rcv", "shot"),
            check_vma=False,
        )(record, shot_fire_samples)

    return step
```

```python
import functools
import math

import jax
import jax.numpy as jnp
from jax import lax
from jax.experimental import pallas as pl
from jax.experimental.pallas import tpu as pltpu
from jax.sharding import PartitionSpec as P

WIN = 2048
SPACING = 256


freq_bins = (24, 40, 56, 80)


def shifted(block, axis, distance):
    devices = range(lax.axis_size(axis))
    route = [(i - distance, i) for i in devices if i - distance in devices]
    return lax.ppermute(block, axis, route)


def dft_table(window_len):
    lag_index = jnp.arange(window_len, dtype=jnp.int32)
    bin_list = jnp.array(freq_bins, dtype=jnp.int32)
    turn_count = lag_index[:, None] * bin_list[None, :] % window_len
    phase_angle = 2.0 * math.pi / window_len * turn_count.astype(jnp.float32)
    dft_rows = jnp.concatenate([jnp.cos(phase_angle), -jnp.sin(phase_angle)], axis=1) / math.sqrt(
        window_len
    )
    return dft_rows.astype(jnp.bfloat16)


def shifted_tables(jitter, span):
    lag_index = jnp.arange(span, dtype=jnp.int32)[None, :] - jitter[:, None]
    inside = (lag_index >= 0) & (lag_index < WIN)
    clipped = jnp.clip(lag_index, 0, WIN - 1)
    bin_list = jnp.array(freq_bins, dtype=jnp.int32)
    turn_count = clipped[:, None, :] * bin_list[None, :, None] % WIN
    phase_angle = 2.0 * math.pi / WIN * turn_count.astype(jnp.float32)
    table = jnp.concatenate([jnp.cos(phase_angle), -jnp.sin(phase_angle)], axis=1) / math.sqrt(WIN)
    table = jnp.where(inside[:, None, :], table, 0.0)
    return table.astype(jnp.bfloat16)


def local_spectra(extended, sample_offsets, dft_rows):
    count_of_shots = sample_offsets.shape[0]
    reach_blocks = WIN // SPACING + 1
    jitter = sample_offsets - jnp.arange(count_of_shots, dtype=jnp.int32) * SPACING
    tables = shifted_tables(jitter, reach_blocks * SPACING)
    tables = tables.reshape(count_of_shots, dft_rows.shape[1], reach_blocks, SPACING)
    blocks = extended.reshape(extended.shape[0], extended.shape[1] // SPACING, SPACING)
    total = jnp.zeros((count_of_shots, dft_rows.shape[1], extended.shape[0]), jnp.float32)
    for offset in range(reach_blocks):
        record_part = blocks[:, offset : offset + count_of_shots, :]
        total = total + jnp.einsum(
            "rsu,scu->scr", record_part, tables[:, :, offset, :], preferred_element_type=jnp.float32
        )
    return total


def gram_terms(left, right):
    nfreq = len(freq_bins)
    left_re = left[:, :nfreq, :]
    left_im = left[:, nfreq:, :]
    right_re = right[:, :nfreq, :]
    right_im = right[:, nfreq:, :]
    gram_real = jnp.einsum("sfr,sfq->frq", left_re, right_re, preferred_element_type=jnp.float32)
    gram_real = gram_real + jnp.einsum(
        "sfr,sfq->frq", left_im, right_im, preferred_element_type=jnp.float32
    )
    gram_imag = jnp.einsum("sfr,sfq->frq", left_re, right_im, preferred_element_type=jnp.float32)
    gram_imag = gram_imag - jnp.einsum(
        "sfr,sfq->frq", left_im, right_re, preferred_element_type=jnp.float32
    )
    return jnp.stack([gram_real, gram_imag], axis=0)


def per_device(record, shot_fire_samples):
    trace_segment_length = record.shape[1]
    count_of_shots = shot_fire_samples.shape[0]
    dft_rows = dft_table(WIN)
    sample_offsets = shot_fire_samples - lax.axis_index("shot") * trace_segment_length
    head_rows = record[:, :WIN]
    rim_rows = shifted(head_rows, "shot", -1)
    extended = jnp.concatenate([record, rim_rows], axis=1)
    trace_spectra = local_spectra(extended, sample_offsets, dft_rows)
    trace_spectra = trace_spectra.astype(jnp.bfloat16)
    all_receivers = lax.all_gather(trace_spectra, "rcv", axis=2, tiled=True)
    total_shots = count_of_shots * lax.axis_size("shot")
    row_side = lax.all_gather(trace_spectra, "shot", axis=0, tiled=True)
    column_side = lax.all_to_all(all_receivers, "shot", split_axis=2, concat_axis=0, tiled=True)
    result = gram_terms(row_side, column_side)
    return result / total_shots


LANES = 128
HALF = 16
GROUP = 8
PIECES = 4
MESH = pl.DeviceIdType.MESH


def lane_fields(shape):
    lane = lax.broadcasted_iota(jnp.int32, shape, len(shape) - 1)
    return lane // 16 % 4, lane // 8 % 2, lane // 64 * 8 + lane % 8


def rotated(lag, quarter):
    freq, part, _ = lane_fields((1, LANES))
    bins = jnp.full((1, LANES), freq_bins[0], jnp.int32)
    for f in range(1, len(freq_bins)):
        bins = jnp.where(freq == f, freq_bins[f], bins)
    turn = (lag & (SPACING - 1)) * bins + (part * quarter[0] + quarter[1]) * (WIN // 4)
    turn = ((turn + WIN // 2) & (WIN - 1)) - WIN // 2
    x = (math.pi / WIN) * turn.astype(jnp.float32)
    y = x * x
    series = 1.0 / math.factorial(13)
    for k in (11, 9, 7, 5, 3, 1):
        series = series * y + (-1.0) ** (k // 2) / math.factorial(k)
    half_sine = x * series
    return 1.0 - 2.0 * half_sine * half_sine


def kernel(
    n, ncol, fire_hbm, rec_ref, out_ref,
    fire_ref, fire_sem, rec, joff, poff, wave, mask, tm0, tmc, tm1, tmf, rim_out, rim_in, gat, col, rmat,
    rec_sem, jit_sem, rim_sem, ring_send, share_send, ring_recv, share_recv, col_send, col_recv,
):
    me = lax.axis_index("shot")
    mj = lax.axis_index("rcv")
    rows = rec.shape[0]
    fold = rows // 2
    span = GROUP * SPACING
    chips = n // 2
    nz = chips // 2
    half = chips // 2
    reach = WIN // SPACING
    core = me % 2
    chip = me // 2
    z, y = chip // 2, chip % 2
    pos = jnp.where(y == 0, z, chips - 1 - z)

    def chip_at(position):
        q = (position + 2 * chips) % chips
        second = q >= nz
        zz = jnp.where(second, chips - 1 - q, q)
        return zz * 2 + jnp.where(second, 1, 0)

    ahead = (chip_at(pos + 1), chip_at(pos - 1))
    pair = chip * 2 + (1 - core)
    has_prev, has_next = me > 0, me < n - 1
    prev, nxt = jnp.maximum(me - 1, 0), jnp.minimum(me + 1, n - 1)

    def load(g):
        part = pl.ds(g * span, span)
        return pltpu.make_async_copy(rec_ref.at[:, part], rec.at[:, part], rec_sem.at[g])

    fires = pltpu.make_async_copy(fire_hbm, fire_ref, fire_sem)
    fires.start()
    for g in range(4):
        load(g).start()

    barrier = pltpu.get_barrier_semaphore()

    def greet(other, column):
        pl.semaphore_signal(barrier, inc=1, device_id=(other, column), device_id_type=MESH)

    pl.when(has_prev)(lambda: greet(prev, mj))
    pl.when(has_next)(lambda: greet(nxt, mj))
    greet(pair, mj)
    for other in ahead:
        greet(other * 2 + core, mj)
    for other in (chip, *ahead):
        for which in range(2):
            greet(other * 2 + which, 1 - mj)
    greeted = 9 + has_prev.astype(jnp.int32) + has_next.astype(jnp.int32)

    freq, part_of, shot_lane = lane_fields((1, LANES))
    lower_lanes = lax.broadcasted_iota(jnp.int32, (1, LANES), 1) < LANES // 2
    row_index = lax.broadcasted_iota(jnp.int32, (SPACING, LANES), 0)
    wave[0] = rotated(row_index, (1, 0)) * (1.0 / math.sqrt(WIN))
    wave[1] = rotated(row_index, (1, -1)) * (1.0 / math.sqrt(WIN))
    for rel in range(3 * GROUP):
        order = rel - lane_fields((16, LANES))[2]
        early = (order >= 0) & (order < reach)
        late = (order >= 1) & (order <= reach)
        mask[0, rel] = early.astype(jnp.float32).astype(jnp.bfloat16)
        mask[1, rel] = late.astype(jnp.float32).astype(jnp.bfloat16)
    out_ref[...] = jnp.zeros_like(out_ref)
    fires.wait()
    jitters = []
    for h in range(2):
        row = jnp.zeros((1, LANES), jnp.int32)
        for s in range(HALF):
            row = jnp.where(shot_lane == s, fire_ref[h * HALF + s], row)
        jitters.append(row & (SPACING - 1))
    joff[...] = jnp.broadcast_to(jitters[1], joff.shape)

    @pl.when(me == 0)
    def _():
        poff[...] = jnp.zeros_like(poff)

    jitter = pltpu.make_async_remote_copy(
        joff, poff, jit_sem.at[0], jit_sem.at[1], device_id=(nxt, mj), device_id_type=MESH
    )
    rim = pltpu.make_async_remote_copy(
        rim_out, rim_in, rim_sem.at[0], rim_sem.at[1], device_id=(prev, mj), device_id_type=MESH
    )

    def fill(start, places):
        turned = rotated(start, (0, 0)), rotated(start, (0, -1))
        for c in range(SPACING // 16):
            part = slice(c * 16, (c + 1) * 16)
            value = wave[0, part] * turned[0] + wave[1, part] * turned[1]
            inside = lax.broadcasted_iota(jnp.int32, (16, LANES), 0) + c * 16 >= start
            early = jnp.where(inside, value, 0.0).astype(jnp.bfloat16)
            late = jnp.where(inside, 0.0, value).astype(jnp.bfloat16)
            for rel, (ref, block, lanes) in places.items():
                at = slice(block * SPACING + c * 16, block * SPACING + (c + 1) * 16)
                ref[at, lanes] = early * mask[0, rel] + late * mask[1, rel]

    low, high = slice(0, LANES), slice(LANES, 2 * LANES)

    def two_dots(block, count, ref, first):
        parts = []
        for k in range(2):
            b, f = block + k * count, first + k * count
            parts.append(
                jnp.dot(
                    rec[:, b * SPACING : (b + count) * SPACING],
                    ref[f * SPACING : (f + count) * SPACING, :],
                    preferred_element_type=jnp.float32,
                )
            )
        return parts[0] + parts[1]

    def folded(value, second):
        top, bottom = value[:fold], value[fold:]
        if second:
            return jnp.where(lower_lanes, pltpu.roll(top, LANES // 2, 1), bottom)
        return jnp.where(lower_lanes, top, pltpu.roll(bottom, LANES // 2, 1))

    def ring(src, p, d):
        return pltpu.make_async_remote_copy(
            gat.at[src, p], gat.at[src, p], ring_send.at[d], ring_recv.at[src // 2, p],
            device_id=(ahead[d] * 2 + core, mj), device_id_type=MESH,
        )

    def share(src, p):
        return pltpu.make_async_remote_copy(
            gat.at[src, p], gat.at[src, p], share_send, share_recv.at[src // 2],
            device_id=(pair, mj), device_id_type=MESH,
        )

    def column_rows(target):
        home = target * 2 * ncol // rows
        first = target * 2 * ncol - home * rows
        top = first // fold
        return home == mj, top, pl.multiple_of(first - top * fold, 16)

    def send_col(src, p, target, sem):
        mine, top, first = column_rows(target)
        wanted = mine & (top == p) if p < 2 else mine

        @pl.when(wanted)
        def _():
            for which in range(2):
                pltpu.make_async_remote_copy(
                    gat.at[src, p, pl.ds(first + which * ncol, ncol), :], col.at[src, max(p - 1, 0)],
                    col_send.at[sem], col_recv.at[src],
                    device_id=(target * 2 + which, 1 - mj), device_id_type=MESH,
                ).start()

    def hops(p, d):
        return half if p % 2 == d else half - 1

    def source(t, d, which):
        return chip_at(pos - t if d == 0 else pos + t) * 2 + which

    def send_own(p):
        for d in (p % 2, 1 - p % 2):
            ring(me, p, d).start()

    def spread(src, p):
        share(src, p).start()
        send_col(src, p, chip, 0)

    def arrive(t, p):
        for d in (p % 2, 1 - p % 2):
            if t > hops(p, d):
                continue
            src = source(t, d, core)
            ring(src, p, d).wait_recv()
            if t < hops(p, d):
                ring(src, p, d).start()
            if t == half - 1 and hops(p, d) == half:
                send_col(src, p, ahead[d], 1 + p)
            if t < half:
                spread(src, p)
            else:
                share(src, p).start()

    provider, col_top, col_first = column_rows(chip)
    own_first = pl.multiple_of(col_first + core * ncol, 16)

    def take(buffer, sem):
        pltpu.make_async_copy(buffer, buffer, sem).wait()

    def gram(src, shared):
        if shared:
            take(gat.at[src], share_recv.at[src // 2])

        @pl.when(provider)
        def _():
            for k, p in enumerate((col_top, 2, 3)):
                col[src, k] = gat[src, p, pl.ds(own_first, ncol), :]

        pl.when(jnp.logical_not(provider))(lambda: take(col.at[src], col_recv.at[src]))
        xa, xb, xc = (col[src, k].astype(jnp.float32) for k in range(3))
        top = col_top == 0
        xb = jnp.where(top, xb, pltpu.roll(xb, LANES // 2, 1))
        xc = jnp.where(top, pltpu.roll(xc, LANES // 2, 1), xc)
        for h, x in enumerate((xa, jnp.where(lower_lanes, xb, xc))):
            swapped = jnp.where(part_of == 0, pltpu.roll(x, LANES - 8, 1), -pltpu.roll(x, 8, 1))
            for ri, value in enumerate((x, swapped)):
                for f in range(4):
                    rmat[pl.ds((ri * 4 + f) * ncol, ncol), h * LANES : (h + 1) * LANES] = jnp.where(
                        freq == f, value, 0.0
                    ).astype(jnp.bfloat16)
        b, c = gat[src, 2], gat[src, 3]
        k = LANES // 2
        left = jnp.concatenate(
            [
                jnp.concatenate([gat[src, 0], b[:, :k], c[:, :k]], axis=1),
                jnp.concatenate([gat[src, 1], b[:, k:], c[:, k:]], axis=1),
            ],
            axis=0,
        )
        out_ref[...] += lax.dot_general(
            rmat[...], left, (((1,), (1,)), ((), ())), preferred_element_type=jnp.float32
        )

    def gram_step(t):
        for which in range(2):
            for d in range(2):
                if d == 1 and t in (0, half):
                    continue
                src = source(t, d, core if which == 0 else 1 - core)
                gram(src, which == 1)

    fill(jitters[0], {r: (tm0, r, low) for r in range(16)})
    fill(jitters[0], {16 + r: (tmc, r, low) for r in range(8)})
    fill(jitters[1], {r: (tmc, r, high) for r in range(8)} | {8 + r: (tm1, r, low) for r in range(8)})
    pl.semaphore_wait(barrier, greeted)
    pl.when(has_next)(jitter.start)
    for g in range(3):
        load(g).wait()
    first_half = two_dots(0, 4, tm0, 0) + two_dots(8, 4, tm0, 8)
    middle = two_dots(16, 4, tmc, 0)
    first_half = (first_half + middle[:, :LANES]).astype(jnp.bfloat16)
    for p in range(2):
        gat[me, p] = first_half[p * fold : (p + 1) * fold]
    for p in range(2):
        send_own(p)
    load(3).wait()
    second_half = middle[:, LANES:] + two_dots(24, 4, tm1, 0)
    gat[me, 2] = folded(second_half, False).astype(jnp.bfloat16)
    pl.when(has_prev)(jitter.wait_recv)
    fill(poff[0:1, :], {16 + r: (tmf, r, low) for r in range(8)})
    rim_out[...] = folded(two_dots(0, 4, tmf, 0), True).astype(jnp.bfloat16)
    pl.when(has_prev)(rim.start)
    send_own(2)
    for p in range(3):
        spread(me, p)
    edge = folded(second_half, True)

    def finish():
        pl.when(has_next)(rim.wait_recv)
        outer = jnp.where(has_next, rim_in[...].astype(jnp.float32), 0.0)
        gat[me, 3] = (edge + outer).astype(jnp.bfloat16)
        send_own(3)
        spread(me, 3)

    pl.when(core == 0)(finish)
    for p in range(2):
        arrive(1, p)
    pl.when(core == 1)(finish)
    arrive(1, 2)
    gram_step(0)
    arrive(1, 3)
    for t in range(2, half + 1):
        for p in range(3):
            arrive(t, p)
        gram_step(t - 1)
        arrive(t, 3)
    gram_step(half)

    out_ref[...] *= 1.0 / (n * 2 * HALF)
    pl.when(has_next)(jitter.wait_send)
    pl.when(has_prev)(rim.wait_send)
    for d in range(2):
        whole, rest = divmod(sum(hops(p, d) for p in range(PIECES)), PIECES)
        take(gat.at[pl.ds(0, whole)], ring_send.at[d])
        if rest:
            take(gat.at[0, pl.ds(0, rest)], ring_send.at[d])
    take(gat.at[pl.ds(0, chips)], share_send)
    pl.when(provider)(lambda: take(col.at[pl.ds(0, 2 * (chips - 1))], col_send.at[0]))
    for p in range(PIECES):
        mine, top, _ = column_rows(ahead[p % 2])
        wanted = mine & (top == p) if p < 2 else mine
        pl.when(wanted)(lambda p=p: take(col.at[0, pl.ds(0, 2)], col_send.at[1 + p]))


def fused_device(n, ncol, record, shot_fire_samples):
    rows, length = record.shape
    chips = n // 2
    shot_fire_samples = pltpu.with_memory_space_constraint(shot_fire_samples, pltpu.HBM)
    gram = pl.pallas_call(
        functools.partial(kernel, n, ncol),
        out_shape=jax.ShapeDtypeStruct((8 * ncol, rows), jnp.float32),
        in_specs=[
            pl.BlockSpec(memory_space=pltpu.HBM),
            pl.BlockSpec(memory_space=pltpu.HBM),
        ],
        out_specs=pl.BlockSpec(memory_space=pltpu.VMEM),
        scratch_shapes=[
            pltpu.SMEM(shot_fire_samples.shape, jnp.int32),
            pltpu.SemaphoreType.DMA,
            pltpu.VMEM((rows, length), jnp.bfloat16),
            pltpu.VMEM((8, LANES), jnp.int32),
            pltpu.VMEM((8, LANES), jnp.int32),
            pltpu.VMEM((2, SPACING, LANES), jnp.float32),
            pltpu.VMEM((2, 3 * GROUP, 16, LANES), jnp.bfloat16),
            pltpu.VMEM((2 * GROUP * SPACING, LANES), jnp.bfloat16),
            pltpu.VMEM((GROUP * SPACING, 2 * LANES), jnp.bfloat16),
            pltpu.VMEM((GROUP * SPACING, LANES), jnp.bfloat16),
            pltpu.VMEM((GROUP * SPACING, LANES), jnp.bfloat16),
            pltpu.VMEM((rows // 2, LANES), jnp.bfloat16),
            pltpu.VMEM((rows // 2, LANES), jnp.bfloat16),
            pltpu.VMEM((n, PIECES, rows // 2, LANES), jnp.bfloat16),
            pltpu.VMEM((n, 3, ncol, LANES), jnp.bfloat16),
            pltpu.VMEM((8 * ncol, 2 * LANES), jnp.bfloat16),
            pltpu.SemaphoreType.DMA((length // (GROUP * SPACING),)),
            pltpu.SemaphoreType.DMA((2,)),
            pltpu.SemaphoreType.DMA((2,)),
            pltpu.SemaphoreType.DMA((2,)),
            pltpu.SemaphoreType.DMA,
            pltpu.SemaphoreType.DMA((chips, PIECES)),
            pltpu.SemaphoreType.DMA((chips,)),
            pltpu.SemaphoreType.DMA((1 + PIECES,)),
            pltpu.SemaphoreType.DMA((n,)),
        ],
        compiler_params=pltpu.CompilerParams(
            collective_id=0, has_side_effects=True, vmem_limit_bytes=50 * 1024 * 1024
        ),
    )(shot_fire_samples, record)
    return gram.reshape(2, 4, ncol, rows).transpose(0, 1, 3, 2)


def whole_step(n, receivers, record, shot_fire_samples):
    rows, length = record.shape
    shots = shot_fire_samples.shape[0]
    ncol = receivers // n
    fits = (
        receivers == 2 * rows and ncol % 16 == 0 and rows % (4 * ncol) == 0
        and shots == 2 * HALF and length == shots * SPACING and n % 8 == 0
    )
    if fits:
        return fused_device(n, ncol, record, shot_fire_samples)
    return per_device(record, shot_fire_samples)


def solution(mesh):
    def step(record, shot_fire_samples):
        body = functools.partial(whole_step, mesh.shape["shot"], record.shape[0])
        return jax.shard_map(
            body,
            mesh=mesh,
            in_specs=(P("rcv", "shot"), P("shot")),
            out_specs=P(None, None, "rcv", "shot"),
            check_vma=False,
        )(record, shot_fire_samples)

    return step
```

```python
import functools
import math

import jax
import jax.numpy as jnp
from jax import lax
from jax.experimental import pallas as pl
from jax.experimental.pallas import tpu as pltpu
from jax.sharding import PartitionSpec as P

WIN = 2048
SPACING = 256


freq_bins = (24, 40, 56, 80)


def shifted(block, axis, distance):
    devices = range(lax.axis_size(axis))
    route = [(i - distance, i) for i in devices if i - distance in devices]
    return lax.ppermute(block, axis, route)


def dft_table(window_len):
    lag_index = jnp.arange(window_len, dtype=jnp.int32)
    bin_list = jnp.array(freq_bins, dtype=jnp.int32)
    turn_count = lag_index[:, None] * bin_list[None, :] % window_len
    phase_angle = 2.0 * math.pi / window_len * turn_count.astype(jnp.float32)
    dft_rows = jnp.concatenate([jnp.cos(phase_angle), -jnp.sin(phase_angle)], axis=1) / math.sqrt(
        window_len
    )
    return dft_rows.astype(jnp.bfloat16)


def shifted_tables(jitter, span):
    lag_index = jnp.arange(span, dtype=jnp.int32)[None, :] - jitter[:, None]
    inside = (lag_index >= 0) & (lag_index < WIN)
    clipped = jnp.clip(lag_index, 0, WIN - 1)
    bin_list = jnp.array(freq_bins, dtype=jnp.int32)
    turn_count = clipped[:, None, :] * bin_list[None, :, None] % WIN
    phase_angle = 2.0 * math.pi / WIN * turn_count.astype(jnp.float32)
    table = jnp.concatenate([jnp.cos(phase_angle), -jnp.sin(phase_angle)], axis=1) / math.sqrt(WIN)
    table = jnp.where(inside[:, None, :], table, 0.0)
    return table.astype(jnp.bfloat16)


def local_spectra(extended, sample_offsets, dft_rows):
    count_of_shots = sample_offsets.shape[0]
    reach_blocks = WIN // SPACING + 1
    jitter = sample_offsets - jnp.arange(count_of_shots, dtype=jnp.int32) * SPACING
    tables = shifted_tables(jitter, reach_blocks * SPACING)
    tables = tables.reshape(count_of_shots, dft_rows.shape[1], reach_blocks, SPACING)
    blocks = extended.reshape(extended.shape[0], extended.shape[1] // SPACING, SPACING)
    total = jnp.zeros((count_of_shots, dft_rows.shape[1], extended.shape[0]), jnp.float32)
    for offset in range(reach_blocks):
        record_part = blocks[:, offset : offset + count_of_shots, :]
        total = total + jnp.einsum(
            "rsu,scu->scr", record_part, tables[:, :, offset, :], preferred_element_type=jnp.float32
        )
    return total


def gram_terms(left, right):
    nfreq = len(freq_bins)
    left_re = left[:, :nfreq, :]
    left_im = left[:, nfreq:, :]
    right_re = right[:, :nfreq, :]
    right_im = right[:, nfreq:, :]
    gram_real = jnp.einsum("sfr,sfq->frq", left_re, right_re, preferred_element_type=jnp.float32)
    gram_real = gram_real + jnp.einsum(
        "sfr,sfq->frq", left_im, right_im, preferred_element_type=jnp.float32
    )
    gram_imag = jnp.einsum("sfr,sfq->frq", left_re, right_im, preferred_element_type=jnp.float32)
    gram_imag = gram_imag - jnp.einsum(
        "sfr,sfq->frq", left_im, right_re, preferred_element_type=jnp.float32
    )
    return jnp.stack([gram_real, gram_imag], axis=0)


def per_device(record, shot_fire_samples):
    trace_segment_length = record.shape[1]
    count_of_shots = shot_fire_samples.shape[0]
    dft_rows = dft_table(WIN)
    sample_offsets = shot_fire_samples - lax.axis_index("shot") * trace_segment_length
    head_rows = record[:, :WIN]
    rim_rows = shifted(head_rows, "shot", -1)
    extended = jnp.concatenate([record, rim_rows], axis=1)
    trace_spectra = local_spectra(extended, sample_offsets, dft_rows)
    trace_spectra = trace_spectra.astype(jnp.bfloat16)
    all_receivers = lax.all_gather(trace_spectra, "rcv", axis=2, tiled=True)
    total_shots = count_of_shots * lax.axis_size("shot")
    row_side = lax.all_gather(trace_spectra, "shot", axis=0, tiled=True)
    column_side = lax.all_to_all(all_receivers, "shot", split_axis=2, concat_axis=0, tiled=True)
    result = gram_terms(row_side, column_side)
    return result / total_shots


LANES = 128
HALF = 16
GROUP = 8
PIECES = 4
MESH = pl.DeviceIdType.MESH


def lane_fields(shape):
    lane = lax.broadcasted_iota(jnp.int32, shape, len(shape) - 1)
    return lane // 16 % 4, lane // 8 % 2, lane // 64 * 8 + lane % 8


def rotated(lag, quarter):
    freq, part, _ = lane_fields((1, LANES))
    bins = jnp.full((1, LANES), freq_bins[0], jnp.int32)
    for f in range(1, len(freq_bins)):
        bins = jnp.where(freq == f, freq_bins[f], bins)
    turn = (lag & (SPACING - 1)) * bins + (part * quarter[0] + quarter[1]) * (WIN // 4)
    turn = ((turn + WIN // 2) & (WIN - 1)) - WIN // 2
    x = (math.pi / WIN) * turn.astype(jnp.float32)
    y = x * x
    series = 1.0 / math.factorial(13)
    for k in (11, 9, 7, 5, 3, 1):
        series = series * y + (-1.0) ** (k // 2) / math.factorial(k)
    half_sine = x * series
    return 1.0 - 2.0 * half_sine * half_sine


def kernel(
    n, ncol, fire_hbm, rec_ref, out_ref,
    fire_ref, fire_sem, rec, joff, poff, wave, mask, tm0, tmc, tm1, tmf, rim_out, rim_in, gat, col, rmat,
    rec_sem, jit_sem, rim_sem, ring_send, share_send, ring_recv, share_recv, col_send, col_recv,
):
    me = lax.axis_index("shot")
    mj = lax.axis_index("rcv")
    rows = rec.shape[0]
    fold = rows // 2
    span = GROUP * SPACING
    chips = n // 2
    nz = chips // 2
    half = chips // 2
    reach = WIN // SPACING
    core = me % 2
    chip = me // 2
    z, y = chip // 2, chip % 2
    pos = jnp.where(y == 0, z, chips - 1 - z)

    def chip_at(position):
        q = (position + 2 * chips) % chips
        second = q >= nz
        zz = jnp.where(second, chips - 1 - q, q)
        return zz * 2 + jnp.where(second, 1, 0)

    ahead = (chip_at(pos + 1), chip_at(pos - 1))
    pair = chip * 2 + (1 - core)
    has_prev, has_next = me > 0, me < n - 1
    prev, nxt = jnp.maximum(me - 1, 0), jnp.minimum(me + 1, n - 1)

    def load(g):
        part = pl.ds(g * span, span)
        return pltpu.make_async_copy(rec_ref.at[:, part], rec.at[:, part], rec_sem.at[g])

    fires = pltpu.make_async_copy(fire_hbm, fire_ref, fire_sem)
    fires.start()
    for g in range(4):
        load(g).start()

    barrier = pltpu.get_barrier_semaphore()

    def greet(other, column):
        pl.semaphore_signal(barrier, inc=1, device_id=(other, column), device_id_type=MESH)

    pl.when(has_prev)(lambda: greet(prev, mj))
    pl.when(has_next)(lambda: greet(nxt, mj))
    greet(pair, mj)
    for other in ahead:
        greet(other * 2 + core, mj)
    for which in range(2):
        greet(chip * 2 + which, 1 - mj)
    greeted = 5 + has_prev.astype(jnp.int32) + has_next.astype(jnp.int32)

    freq, part_of, shot_lane = lane_fields((1, LANES))
    lower_lanes = lax.broadcasted_iota(jnp.int32, (1, LANES), 1) < LANES // 2
    row_index = lax.broadcasted_iota(jnp.int32, (16, LANES), 0)
    fine = [rotated(row_index, (1, quarter)) * (1.0 / math.sqrt(WIN)) for quarter in (0, -1)]
    coarse = [rotated(row_index * 16, (0, quarter)) for quarter in (0, -1)]
    for c in range(SPACING // 16):
        at, (cosine, sine) = slice(c * 16, (c + 1) * 16), (turn[c : c + 1] for turn in coarse)
        wave[0, at] = fine[0] * cosine - fine[1] * sine
        wave[1, at] = fine[1] * cosine + fine[0] * sine
    for rel in range(3 * GROUP):
        order = rel - lane_fields((16, LANES))[2]
        early = (order >= 0) & (order < reach)
        late = (order >= 1) & (order <= reach)
        mask[0, rel] = early.astype(jnp.float32).astype(jnp.bfloat16)
        mask[1, rel] = late.astype(jnp.float32).astype(jnp.bfloat16)
    out_ref[...] = jnp.zeros_like(out_ref)
    fires.wait()
    jitters = []
    for h in range(2):
        row = jnp.zeros((1, LANES), jnp.int32)
        for s in range(HALF):
            row = jnp.where(shot_lane == s, fire_ref[h * HALF + s], row)
        jitters.append(row & (SPACING - 1))
    joff[...] = jnp.broadcast_to(jitters[1], joff.shape)

    @pl.when(me == 0)
    def _():
        poff[...] = jnp.zeros_like(poff)

    jitter = pltpu.make_async_remote_copy(
        joff, poff, jit_sem.at[0], jit_sem.at[1], device_id=(nxt, mj), device_id_type=MESH
    )
    rim = pltpu.make_async_remote_copy(
        rim_out, rim_in, rim_sem.at[0], rim_sem.at[1], device_id=(prev, mj), device_id_type=MESH
    )

    def fill(start, places):
        turned = rotated(start, (0, 0)), rotated(start, (0, -1))
        for c in range(SPACING // 16):
            part = slice(c * 16, (c + 1) * 16)
            value = wave[0, part] * turned[0] + wave[1, part] * turned[1]
            inside = lax.broadcasted_iota(jnp.int32, (16, LANES), 0) + c * 16 >= start
            early = jnp.where(inside, value, 0.0).astype(jnp.bfloat16)
            late = jnp.where(inside, 0.0, value).astype(jnp.bfloat16)
            for rel, (ref, block, lanes) in places.items():
                at = slice(block * SPACING + c * 16, block * SPACING + (c + 1) * 16)
                ref[at, lanes] = early * mask[0, rel] + late * mask[1, rel]

    low, high = slice(0, LANES), slice(LANES, 2 * LANES)

    def two_dots(block, count, ref, first):
        parts = []
        for k in range(2):
            b, f = block + k * count, first + k * count
            parts.append(
                jnp.dot(
                    rec[:, b * SPACING : (b + count) * SPACING],
                    ref[f * SPACING : (f + count) * SPACING, :],
                    preferred_element_type=jnp.float32,
                )
            )
        return parts[0] + parts[1]

    def folded(value, second):
        top, bottom = value[:fold], value[fold:]
        if second:
            return jnp.where(lower_lanes, pltpu.roll(top, LANES // 2, 1), bottom)
        return jnp.where(lower_lanes, top, pltpu.roll(bottom, LANES // 2, 1))

    def ring(src, p, d):
        return pltpu.make_async_remote_copy(
            gat.at[src, p], gat.at[src, p], ring_send.at[d], ring_recv.at[src // 2, p],
            device_id=(ahead[d] * 2 + core, mj), device_id_type=MESH,
        )

    def share(src, p):
        return pltpu.make_async_remote_copy(
            gat.at[src, p], gat.at[src, p], share_send, share_recv.at[src // 2],
            device_id=(pair, mj), device_id_type=MESH,
        )

    def column_rows(target):
        home = target * 2 * ncol // rows
        first = target * 2 * ncol - home * rows
        top = first // fold
        return home == mj, top, pl.multiple_of(first - top * fold, 16)

    def send_col(src, p, target, sem):
        mine, top, first = column_rows(target)
        wanted = mine & (top == p) if p < 2 else mine

        @pl.when(wanted)
        def _():
            for which in range(2):
                pltpu.make_async_remote_copy(
                    gat.at[src, p, pl.ds(first + which * ncol, ncol), :], col.at[src, max(p - 1, 0)],
                    col_send.at[sem], col_recv.at[src],
                    device_id=(target * 2 + which, 1 - mj), device_id_type=MESH,
                ).start()

    def hops(p, d):
        return half if p % 2 == d else half - 1

    def source(t, d, which):
        return chip_at(pos - t if d == 0 else pos + t) * 2 + which

    def send_own(p):
        for d in (p % 2, 1 - p % 2):
            ring(me, p, d).start()

    def spread(src, p):
        share(src, p).start()
        send_col(src, p, chip, 0)

    def arrive(t, p, d):
        src = source(t, d, core)
        ring(src, p, d).wait_recv()
        if t < hops(p, d):
            ring(src, p, d).start()
        if t == half - 1 and hops(p, d) == half:
            send_col(src, p, ahead[d], 1 + p)
        if t < half:
            spread(src, p)
        else:
            share(src, p).start()

    provider, col_top, col_first = column_rows(chip)
    own_first = pl.multiple_of(col_first + core * ncol, 16)

    def take(buffer, sem):
        pltpu.make_async_copy(buffer, buffer, sem).wait()

    def gram(sources, last=False):
        for src, shared in sources:
            if shared:
                take(gat.at[src], share_recv.at[src // 2])

        @pl.when(provider)
        def _():
            for src, _ in sources:
                for k, p in enumerate((col_top, 2, 3)):
                    col[src, k] = gat[src, p, pl.ds(own_first, ncol), :]

        @pl.when(jnp.logical_not(provider))
        def _():
            for src, _ in sources:
                take(col.at[src], col_recv.at[src])

        lefts = []
        for slot, (src, _) in enumerate(sources):
            xa, xb, xc = (col[src, k].astype(jnp.float32) for k in range(3))
            top = col_top == 0
            xb = jnp.where(top, xb, pltpu.roll(xb, LANES // 2, 1))
            xc = jnp.where(top, pltpu.roll(xc, LANES // 2, 1), xc)
            for h, x in enumerate((xa, jnp.where(lower_lanes, xb, xc))):
                at = slice((2 * slot + h) * LANES, (2 * slot + h + 1) * LANES)
                swapped = jnp.where(part_of == 0, pltpu.roll(x, LANES - 8, 1), -pltpu.roll(x, 8, 1))
                for ri, value in enumerate((x, swapped)):
                    for f in range(4):
                        rmat[pl.ds((ri * 4 + f) * ncol, ncol), at] = jnp.where(
                            freq == f, value, 0.0
                        ).astype(jnp.bfloat16)
            b, c = gat[src, 2], gat[src, 3]
            k = LANES // 2
            lefts.append(
                jnp.concatenate(
                    [
                        jnp.concatenate([gat[src, 0], b[:, :k], c[:, :k]], axis=1),
                        jnp.concatenate([gat[src, 1], b[:, k:], c[:, k:]], axis=1),
                    ],
                    axis=0,
                )
            )
        total = out_ref[...] + lax.dot_general(
            rmat[:, : 2 * LANES * len(sources)], jnp.concatenate(lefts, axis=1),
            (((1,), (1,)), ((), ())), preferred_element_type=jnp.float32,
        )
        out_ref[...] = total * (1.0 / (n * 2 * HALF)) if last else total

    def grams(t):
        found = []
        for other in range(2):
            for d in range(2):
                if d == 1 and t in (0, half):
                    continue
                found.append((source(t, d, 1 - core if other else core), other == 1))
        return found

    fill(jitters[0], {r: (tm0, r, low) for r in range(16)})
    fill(jitters[0], {16 + r: (tmc, r, low) for r in range(8)})
    fill(jitters[1], {r: (tmc, r, high) for r in range(8)} | {8 + r: (tm1, r, low) for r in range(8)})
    pl.semaphore_wait(barrier, greeted)
    pl.when(has_next)(jitter.start)
    for g in range(3):
        load(g).wait()
    first_half = two_dots(0, 4, tm0, 0) + two_dots(8, 4, tm0, 8)
    middle = two_dots(16, 4, tmc, 0)
    first_half = (first_half + middle[:, :LANES]).astype(jnp.bfloat16)
    for p in range(2):
        gat[me, p] = first_half[p * fold : (p + 1) * fold]
    for p in range(2):
        send_own(p)
    load(3).wait()
    second_half = middle[:, LANES:] + two_dots(24, 4, tm1, 0)
    gat[me, 2] = folded(second_half, False).astype(jnp.bfloat16)
    pl.when(has_prev)(jitter.wait_recv)
    fill(poff[0:1, :], {16 + r: (tmf, r, low) for r in range(8)})
    rim_out[...] = folded(out_ref[:, :LANES] + two_dots(0, 4, tmf, 0), True).astype(jnp.bfloat16)
    pl.when(has_prev)(rim.start)
    send_own(2)
    for p in range(3):
        spread(me, p)
    edge = folded(second_half, True)

    def finish():
        pl.when(has_next)(rim.wait_recv)
        outer = jnp.where(has_next, rim_in[...].astype(jnp.float32), 0.0)
        gat[me, 3] = (edge + outer).astype(jnp.bfloat16)
        send_own(3)
        spread(me, 3)

    def arrivals(t, p):
        for d in (p % 2, 1 - p % 2):
            if t <= hops(p, d):
                arrive(t, p, d)

    pl.when(core == 0)(finish)
    for p in range(2):
        arrivals(1, p)
    pl.when(core == 1)(finish)
    arrivals(1, 2)
    gram(grams(0))
    arrivals(1, 3)
    for t in range(2, half + 1):
        for p in range(3):
            arrivals(t, p)
        gram(grams(t - 1))
        arrivals(t, 3)
    own, other = grams(half)
    gram([own])
    gram([other], last=True)

    pl.when(has_next)(jitter.wait_send)
    pl.when(has_prev)(rim.wait_send)
    for d in range(2):
        whole, rest = divmod(sum(hops(p, d) for p in range(PIECES)), PIECES)
        take(gat.at[pl.ds(0, whole)], ring_send.at[d])
        if rest:
            take(gat.at[0, pl.ds(0, rest)], ring_send.at[d])
    take(gat.at[pl.ds(0, chips)], share_send)
    pl.when(provider)(lambda: take(col.at[pl.ds(0, 2 * (chips - 1))], col_send.at[0]))
    for p in range(PIECES):
        mine, top, _ = column_rows(ahead[p % 2])
        wanted = mine & (top == p) if p < 2 else mine
        pl.when(wanted)(lambda p=p: take(col.at[0, pl.ds(0, 2)], col_send.at[1 + p]))


def fused_device(n, ncol, record, shot_fire_samples):
    rows, length = record.shape
    chips = n // 2
    shot_fire_samples = pltpu.with_memory_space_constraint(shot_fire_samples, pltpu.HBM)
    gram = pl.pallas_call(
        functools.partial(kernel, n, ncol),
        out_shape=jax.ShapeDtypeStruct((8 * ncol, rows), jnp.float32),
        in_specs=[
            pl.BlockSpec(memory_space=pltpu.HBM),
            pl.BlockSpec(memory_space=pltpu.HBM),
        ],
        out_specs=pl.BlockSpec(memory_space=pltpu.VMEM),
        scratch_shapes=[
            pltpu.SMEM(shot_fire_samples.shape, jnp.int32),
            pltpu.SemaphoreType.DMA,
            pltpu.VMEM((rows, length), jnp.bfloat16),
            pltpu.VMEM((8, LANES), jnp.int32),
            pltpu.VMEM((8, LANES), jnp.int32),
            pltpu.VMEM((2, SPACING, LANES), jnp.float32),
            pltpu.VMEM((2, 3 * GROUP, 16, LANES), jnp.bfloat16),
            pltpu.VMEM((2 * GROUP * SPACING, LANES), jnp.bfloat16),
            pltpu.VMEM((GROUP * SPACING, 2 * LANES), jnp.bfloat16),
            pltpu.VMEM((GROUP * SPACING, LANES), jnp.bfloat16),
            pltpu.VMEM((GROUP * SPACING, LANES), jnp.bfloat16),
            pltpu.VMEM((rows // 2, LANES), jnp.bfloat16),
            pltpu.VMEM((rows // 2, LANES), jnp.bfloat16),
            pltpu.VMEM((n, PIECES, rows // 2, LANES), jnp.bfloat16),
            pltpu.VMEM((n, 3, ncol, LANES), jnp.bfloat16),
            pltpu.VMEM((8 * ncol, 8 * LANES), jnp.bfloat16),
            pltpu.SemaphoreType.DMA((length // (GROUP * SPACING),)),
            pltpu.SemaphoreType.DMA((2,)),
            pltpu.SemaphoreType.DMA((2,)),
            pltpu.SemaphoreType.DMA((2,)),
            pltpu.SemaphoreType.DMA,
            pltpu.SemaphoreType.DMA((chips, PIECES)),
            pltpu.SemaphoreType.DMA((chips,)),
            pltpu.SemaphoreType.DMA((1 + PIECES,)),
            pltpu.SemaphoreType.DMA((n,)),
        ],
        compiler_params=pltpu.CompilerParams(
            collective_id=0, has_side_effects=True, vmem_limit_bytes=50 * 1024 * 1024
        ),
    )(shot_fire_samples, record)
    return gram.reshape(2, 4, ncol, rows).transpose(0, 1, 3, 2)


def whole_step(n, receivers, record, shot_fire_samples):
    rows, length = record.shape
    shots = shot_fire_samples.shape[0]
    ncol = receivers // n
    fits = (
        receivers == 2 * rows and ncol % 16 == 0 and rows % (4 * ncol) == 0
        and shots == 2 * HALF and length == shots * SPACING and n % 8 == 0
    )
    if fits:
        return fused_device(n, ncol, record, shot_fire_samples)
    return per_device(record, shot_fire_samples)


def solution(mesh):
    def step(record, shot_fire_samples):
        body = functools.partial(whole_step, mesh.shape["shot"], record.shape[0])
        return jax.shard_map(
            body,
            mesh=mesh,
            in_specs=(P("rcv", "shot"), P("shot")),
            out_specs=P(None, None, "rcv", "shot"),
            check_vma=False,
        )(record, shot_fire_samples)

    return step
```

```python
import functools
import math

import jax
import jax.numpy as jnp
from jax import lax
from jax.experimental import pallas as pl
from jax.experimental.pallas import tpu as pltpu
from jax.sharding import PartitionSpec as P

WIN = 2048
SPACING = 256


freq_bins = (24, 40, 56, 80)


def shifted(block, axis, distance):
    devices = range(lax.axis_size(axis))
    route = [(i - distance, i) for i in devices if i - distance in devices]
    return lax.ppermute(block, axis, route)


def dft_table(window_len):
    lag_index = jnp.arange(window_len, dtype=jnp.int32)
    bin_list = jnp.array(freq_bins, dtype=jnp.int32)
    turn_count = lag_index[:, None] * bin_list[None, :] % window_len
    phase_angle = 2.0 * math.pi / window_len * turn_count.astype(jnp.float32)
    dft_rows = jnp.concatenate([jnp.cos(phase_angle), -jnp.sin(phase_angle)], axis=1) / math.sqrt(
        window_len
    )
    return dft_rows.astype(jnp.bfloat16)


def shifted_tables(jitter, span):
    lag_index = jnp.arange(span, dtype=jnp.int32)[None, :] - jitter[:, None]
    inside = (lag_index >= 0) & (lag_index < WIN)
    clipped = jnp.clip(lag_index, 0, WIN - 1)
    bin_list = jnp.array(freq_bins, dtype=jnp.int32)
    turn_count = clipped[:, None, :] * bin_list[None, :, None] % WIN
    phase_angle = 2.0 * math.pi / WIN * turn_count.astype(jnp.float32)
    table = jnp.concatenate([jnp.cos(phase_angle), -jnp.sin(phase_angle)], axis=1) / math.sqrt(WIN)
    table = jnp.where(inside[:, None, :], table, 0.0)
    return table.astype(jnp.bfloat16)


def local_spectra(extended, sample_offsets, dft_rows):
    count_of_shots = sample_offsets.shape[0]
    reach_blocks = WIN // SPACING + 1
    jitter = sample_offsets - jnp.arange(count_of_shots, dtype=jnp.int32) * SPACING
    tables = shifted_tables(jitter, reach_blocks * SPACING)
    tables = tables.reshape(count_of_shots, dft_rows.shape[1], reach_blocks, SPACING)
    blocks = extended.reshape(extended.shape[0], extended.shape[1] // SPACING, SPACING)
    total = jnp.zeros((count_of_shots, dft_rows.shape[1], extended.shape[0]), jnp.float32)
    for offset in range(reach_blocks):
        record_part = blocks[:, offset : offset + count_of_shots, :]
        total = total + jnp.einsum(
            "rsu,scu->scr", record_part, tables[:, :, offset, :], preferred_element_type=jnp.float32
        )
    return total


def gram_terms(left, right):
    nfreq = len(freq_bins)
    left_re = left[:, :nfreq, :]
    left_im = left[:, nfreq:, :]
    right_re = right[:, :nfreq, :]
    right_im = right[:, nfreq:, :]
    gram_real = jnp.einsum("sfr,sfq->frq", left_re, right_re, preferred_element_type=jnp.float32)
    gram_real = gram_real + jnp.einsum(
        "sfr,sfq->frq", left_im, right_im, preferred_element_type=jnp.float32
    )
    gram_imag = jnp.einsum("sfr,sfq->frq", left_re, right_im, preferred_element_type=jnp.float32)
    gram_imag = gram_imag - jnp.einsum(
        "sfr,sfq->frq", left_im, right_re, preferred_element_type=jnp.float32
    )
    return jnp.stack([gram_real, gram_imag], axis=0)


def per_device(record, shot_fire_samples):
    trace_segment_length = record.shape[1]
    count_of_shots = shot_fire_samples.shape[0]
    dft_rows = dft_table(WIN)
    sample_offsets = shot_fire_samples - lax.axis_index("shot") * trace_segment_length
    head_rows = record[:, :WIN]
    rim_rows = shifted(head_rows, "shot", -1)
    extended = jnp.concatenate([record, rim_rows], axis=1)
    trace_spectra = local_spectra(extended, sample_offsets, dft_rows)
    trace_spectra = trace_spectra.astype(jnp.bfloat16)
    all_receivers = lax.all_gather(trace_spectra, "rcv", axis=2, tiled=True)
    total_shots = count_of_shots * lax.axis_size("shot")
    row_side = lax.all_gather(trace_spectra, "shot", axis=0, tiled=True)
    column_side = lax.all_to_all(all_receivers, "shot", split_axis=2, concat_axis=0, tiled=True)
    result = gram_terms(row_side, column_side)
    return result / total_shots


LANES = 128
HALF = 16
GROUP = 8
PIECES = 4
MESH = pl.DeviceIdType.MESH


def lane_fields(shape):
    lane = lax.broadcasted_iota(jnp.int32, shape, len(shape) - 1)
    return lane // 16 % 4, lane // 8 % 2, lane // 64 * 8 + lane % 8


def rotated(lag, quarter):
    freq, part, _ = lane_fields((1, LANES))
    bins = jnp.full((1, LANES), freq_bins[0], jnp.int32)
    for f in range(1, len(freq_bins)):
        bins = jnp.where(freq == f, freq_bins[f], bins)
    turn = (lag & (SPACING - 1)) * bins + (part * quarter[0] + quarter[1]) * (WIN // 4)
    turn = ((turn + WIN // 2) & (WIN - 1)) - WIN // 2
    x = (math.pi / WIN) * turn.astype(jnp.float32)
    y = x * x
    series = 1.0 / math.factorial(13)
    for k in (11, 9, 7, 5, 3, 1):
        series = series * y + (-1.0) ** (k // 2) / math.factorial(k)
    half_sine = x * series
    return 1.0 - 2.0 * half_sine * half_sine


EVENTS = (
    ('own', 0),
    ('arr', 1, 0, 1),
    ('arr', 1, 0, 0),
    ('own', 1),
    ('arr', 1, 2, 0),
    ('arr', 1, 1, 1),
    ('arr', 1, 1, 0),
    ('arr', 1, 3, 1),
    ('arr', 2, 0, 0),
    ('arr', 1, 2, 1),
    ('arr', 1, 3, 0),
    ('arr', 2, 0, 1),
    ('arr', 2, 1, 1),
    ('gram', ((0, 0, 1),)),
    ('arr', 2, 2, 0),
    ('arr', 2, 1, 0),
    ('gram', ((0, 0, 0),)),
    ('arr', 2, 3, 1),
    ('arr', 2, 3, 0),
    ('arr', 2, 2, 1),
    ('arr', 3, 0, 1),
    ('arr', 3, 0, 0),
    ('arr', 3, 1, 1),
    ('arr', 3, 2, 0),
    ('gram', ((2, 0, 0),)),
    ('arr', 3, 3, 1),
    ('gram', ((1, 0, 1), (1, 1, 0), (2, 0, 1), (2, 1, 0))),
    ('arr', 3, 2, 1),
    ('arr', 3, 1, 0),
    ('arr', 3, 3, 0),
    ('gram', ((1, 1, 1), (2, 1, 1), (1, 0, 0))),
    ('arr', 4, 0, 0),
    ('gram', ((3, 1, 0), (3, 1, 1))),
    ('arr', 4, 1, 1),
    ('arr', 4, 2, 0),
    ('arr', 4, 3, 1),
    ('gram', ((4, 0, 0), (3, 0, 0), (3, 0, 1))),
    ('gram', ((4, 0, 1),)),
)


def plain_events(half):
    def legs(t, p):
        return [("arr", t, p, d) for d in (p % 2, 1 - p % 2) if t <= (half if p % 2 == d else half - 1)]

    def sums(t):
        sides = (0,) if t in (0, half) else (0, 1)
        return tuple((t, d, other) for other in range(2) for d in sides)

    events = [("own", 0), *legs(1, 0), *legs(1, 1), ("own", 1), *legs(1, 2), ("gram", sums(0)), *legs(1, 3)]
    for t in range(2, half + 1):
        events += [*legs(t, 0), *legs(t, 1), *legs(t, 2), ("gram", sums(t - 1)), *legs(t, 3)]
    return [*events, *(("gram", (one,)) for one in sums(half))]


def kernel(
    n, ncol, fire_hbm, rec_ref, out_ref,
    fire_ref, fire_sem, rec, joff, poff, wave, mask, tm0, tmc, tm1, tmf, rim_out, rim_in, gat, col, rmat,
    rec_sem, jit_sem, rim_sem, ring_send, share_send, ring_recv, share_recv, col_send, col_recv,
):
    me = lax.axis_index("shot")
    mj = lax.axis_index("rcv")
    rows = rec.shape[0]
    fold = rows // 2
    span = GROUP * SPACING
    chips = n // 2
    nz = chips // 2
    half = chips // 2
    reach = WIN // SPACING
    core = me % 2
    chip = me // 2
    z, y = chip // 2, chip % 2
    pos = jnp.where(y == 0, z, chips - 1 - z)

    def chip_at(position):
        q = (position + 2 * chips) % chips
        second = q >= nz
        zz = jnp.where(second, chips - 1 - q, q)
        return zz * 2 + jnp.where(second, 1, 0)

    ahead = (chip_at(pos + 1), chip_at(pos - 1))
    pair = chip * 2 + (1 - core)
    has_prev, has_next = me > 0, me < n - 1
    prev, nxt = jnp.maximum(me - 1, 0), jnp.minimum(me + 1, n - 1)

    def load(g):
        part = pl.ds(g * span, span)
        return pltpu.make_async_copy(rec_ref.at[:, part], rec.at[:, part], rec_sem.at[g])

    fires = pltpu.make_async_copy(fire_hbm, fire_ref, fire_sem)
    fires.start()
    for g in range(3):
        load(g).start()

    barrier = pltpu.get_barrier_semaphore()

    def greet(other, column):
        pl.semaphore_signal(barrier, inc=1, device_id=(other, column), device_id_type=MESH)

    pl.when(has_prev)(lambda: greet(prev, mj))
    pl.when(has_next)(lambda: greet(nxt, mj))
    greet(pair, mj)
    for other in ahead:
        greet(other * 2 + core, mj)
    for which in range(2):
        greet(chip * 2 + which, 1 - mj)
    greeted = 5 + has_prev.astype(jnp.int32) + has_next.astype(jnp.int32)

    freq, part_of, shot_lane = lane_fields((1, LANES))
    lower_lanes = lax.broadcasted_iota(jnp.int32, (1, LANES), 1) < LANES // 2
    row_index = lax.broadcasted_iota(jnp.int32, (16, LANES), 0)
    fine = [rotated(row_index, (1, quarter)) * (1.0 / math.sqrt(WIN)) for quarter in (0, -1)]
    coarse = [rotated(row_index * 16, (0, quarter)) for quarter in (0, -1)]
    for c in range(SPACING // 16):
        at, (cosine, sine) = slice(c * 16, (c + 1) * 16), (turn[c : c + 1] for turn in coarse)
        wave[0, at] = fine[0] * cosine - fine[1] * sine
        wave[1, at] = fine[1] * cosine + fine[0] * sine
    for rel in range(3 * GROUP):
        order = rel - lane_fields((16, LANES))[2]
        early = (order >= 0) & (order < reach)
        late = (order >= 1) & (order <= reach)
        mask[0, rel] = early.astype(jnp.float32).astype(jnp.bfloat16)
        mask[1, rel] = late.astype(jnp.float32).astype(jnp.bfloat16)
    out_ref[...] = jnp.zeros_like(out_ref)
    fires.wait()
    jitters = []
    for h in range(2):
        row = jnp.zeros((1, LANES), jnp.int32)
        for s in range(HALF):
            row = jnp.where(shot_lane == s, fire_ref[h * HALF + s], row)
        jitters.append(row & (SPACING - 1))
    joff[...] = jnp.broadcast_to(jitters[1], joff.shape)

    @pl.when(me == 0)
    def _():
        poff[...] = jnp.zeros_like(poff)

    jitter = pltpu.make_async_remote_copy(
        joff, poff, jit_sem.at[0], jit_sem.at[1], device_id=(nxt, mj), device_id_type=MESH
    )
    rim = pltpu.make_async_remote_copy(
        rim_out, rim_in, rim_sem.at[0], rim_sem.at[1], device_id=(prev, mj), device_id_type=MESH
    )

    def fill(start, places):
        turned = rotated(start, (0, 0)), rotated(start, (0, -1))
        for c in range(SPACING // 16):
            part = slice(c * 16, (c + 1) * 16)
            value = wave[0, part] * turned[0] + wave[1, part] * turned[1]
            inside = lax.broadcasted_iota(jnp.int32, (16, LANES), 0) + c * 16 >= start
            early = jnp.where(inside, value, 0.0).astype(jnp.bfloat16)
            late = jnp.where(inside, 0.0, value).astype(jnp.bfloat16)
            for rel, (ref, block, lanes) in places.items():
                at = slice(block * SPACING + c * 16, block * SPACING + (c + 1) * 16)
                ref[at, lanes] = early * mask[0, rel] + late * mask[1, rel]

    low, high = slice(0, LANES), slice(LANES, 2 * LANES)

    def two_dots(block, count, ref, first):
        parts = []
        for k in range(2):
            b, f = block + k * count, first + k * count
            parts.append(
                jnp.dot(
                    rec[:, b * SPACING : (b + count) * SPACING],
                    ref[f * SPACING : (f + count) * SPACING, :],
                    preferred_element_type=jnp.float32,
                )
            )
        return parts[0] + parts[1]

    def folded(value, second):
        top, bottom = value[:fold], value[fold:]
        if second:
            return jnp.where(lower_lanes, pltpu.roll(top, LANES // 2, 1), bottom)
        return jnp.where(lower_lanes, top, pltpu.roll(bottom, LANES // 2, 1))

    def ring(src, p, d):
        return pltpu.make_async_remote_copy(
            gat.at[src, p], gat.at[src, p], ring_send.at[d], ring_recv.at[src // 2, p],
            device_id=(ahead[d] * 2 + core, mj), device_id_type=MESH,
        )

    def share(src, p):
        return pltpu.make_async_remote_copy(
            gat.at[src, p], gat.at[src, p], share_send, share_recv.at[src // 2],
            device_id=(pair, mj), device_id_type=MESH,
        )

    def column_rows(target):
        home = target * 2 * ncol // rows
        first = target * 2 * ncol - home * rows
        top = first // fold
        return home == mj, top, pl.multiple_of(first - top * fold, 16)

    def send_col(src, p, target, sem):
        mine, top, first = column_rows(target)
        wanted = mine & (top == p) if p < 2 else mine

        @pl.when(wanted)
        def _():
            for which in range(2):
                pltpu.make_async_remote_copy(
                    gat.at[src, p, pl.ds(first + which * ncol, ncol), :], col.at[src, max(p - 1, 0)],
                    col_send.at[sem], col_recv.at[src],
                    device_id=(target * 2 + which, 1 - mj), device_id_type=MESH,
                ).start()

    def hops(p, d):
        return half if p % 2 == d else half - 1

    def source(t, d, which):
        return chip_at(pos - t if d == 0 else pos + t) * 2 + which

    def send_own(p):
        for d in (p % 2, 1 - p % 2):
            ring(me, p, d).start()

    def spread(src, p):
        share(src, p).start()
        send_col(src, p, chip, 0)

    def arrive(t, p, d):
        src = source(t, d, core)
        ring(src, p, d).wait_recv()
        if t < hops(p, d):
            ring(src, p, d).start()
        if t == half - 1 and hops(p, d) == half:
            send_col(src, p, ahead[d], 1 + p)
        if t < half:
            spread(src, p)
        else:
            share(src, p).start()

    provider, col_top, col_first = column_rows(chip)
    own_first = pl.multiple_of(col_first + core * ncol, 16)

    def take(buffer, sem):
        pltpu.make_async_copy(buffer, buffer, sem).wait()

    def gram(sources, last=False):
        for src, shared in sources:
            if shared:
                take(gat.at[src], share_recv.at[src // 2])

        @pl.when(provider)
        def _():
            for src, _ in sources:
                for k, p in enumerate((col_top, 2, 3)):
                    col[src, k] = gat[src, p, pl.ds(own_first, ncol), :]

        @pl.when(jnp.logical_not(provider))
        def _():
            for src, _ in sources:
                take(col.at[src], col_recv.at[src])

        lefts = []
        for slot, (src, _) in enumerate(sources):
            xa, xb, xc = (col[src, k].astype(jnp.float32) for k in range(3))
            top = col_top == 0
            xb = jnp.where(top, xb, pltpu.roll(xb, LANES // 2, 1))
            xc = jnp.where(top, pltpu.roll(xc, LANES // 2, 1), xc)
            for h, x in enumerate((xa, jnp.where(lower_lanes, xb, xc))):
                at = slice((2 * slot + h) * LANES, (2 * slot + h + 1) * LANES)
                swapped = jnp.where(part_of == 0, pltpu.roll(x, LANES - 8, 1), -pltpu.roll(x, 8, 1))
                for ri, value in enumerate((x, swapped)):
                    for f in range(4):
                        rmat[pl.ds((ri * 4 + f) * ncol, ncol), at] = jnp.where(
                            freq == f, value, 0.0
                        ).astype(jnp.bfloat16)
            b, c = gat[src, 2], gat[src, 3]
            k = LANES // 2
            lefts.append(
                jnp.concatenate(
                    [
                        jnp.concatenate([gat[src, 0], b[:, :k], c[:, :k]], axis=1),
                        jnp.concatenate([gat[src, 1], b[:, k:], c[:, k:]], axis=1),
                    ],
                    axis=0,
                )
            )
        total = out_ref[...] + lax.dot_general(
            rmat[:, : 2 * LANES * len(sources)], jnp.concatenate(lefts, axis=1),
            (((1,), (1,)), ((), ())), preferred_element_type=jnp.float32,
        )
        out_ref[...] = total * (1.0 / (n * 2 * HALF)) if last else total

    def grams(t):
        found = []
        for other in range(2):
            for d in range(2):
                if d == 1 and t in (0, half):
                    continue
                found.append((source(t, d, 1 - core if other else core), other == 1))
        return found

    fill(jitters[0], {r: (tm0, r, low) for r in range(16)})
    fill(jitters[0], {16 + r: (tmc, r, low) for r in range(8)})
    fill(jitters[1], {r: (tmc, r, high) for r in range(8)} | {8 + r: (tm1, r, low) for r in range(8)})
    load(3).start()
    pl.semaphore_wait(barrier, greeted)
    pl.when(has_next)(jitter.start)
    load(0).wait()
    first_half = two_dots(0, 4, tm0, 0)
    for g in (1, 2):
        load(g).wait()
    first_half = first_half + two_dots(8, 4, tm0, 8)
    middle = two_dots(16, 4, tmc, 0)
    first_half = (first_half + middle[:, :LANES]).astype(jnp.bfloat16)
    for p in range(2):
        gat[me, p] = first_half[p * fold : (p + 1) * fold]
    for p in range(2):
        send_own(p)
    load(3).wait()
    second_half = middle[:, LANES:] + two_dots(24, 4, tm1, 0)
    gat[me, 2] = folded(second_half, False).astype(jnp.bfloat16)
    pl.when(has_prev)(jitter.wait_recv)
    fill(poff[0:1, :], {16 + r: (tmf, r, low) for r in range(8)})
    rim_out[...] = folded(out_ref[:, :LANES] + two_dots(0, 4, tmf, 0), True).astype(jnp.bfloat16)
    pl.when(has_prev)(rim.start)
    send_own(2)
    for p in range(3):
        spread(me, p)
    edge = folded(second_half, True)

    def finish():
        pl.when(has_next)(rim.wait_recv)
        outer = jnp.where(has_next, rim_in[...].astype(jnp.float32), 0.0)
        gat[me, 3] = (edge + outer).astype(jnp.bfloat16)
        send_own(3)
        spread(me, 3)

    def arrivals(t, p):
        for d in (p % 2, 1 - p % 2):
            if t <= hops(p, d):
                arrive(t, p, d)

    events = EVENTS if half == 4 else plain_events(half)
    for event in events:
        if event[0] == "own":
            pl.when(core == event[1])(finish)
        elif event[0] == "arr":
            arrive(*event[1:])
        else:
            group = [(source(t, d, 1 - core if other else core), other == 1) for t, d, other in event[1]]
            gram(group, last=event is events[-1])

    pl.when(has_next)(jitter.wait_send)
    pl.when(has_prev)(rim.wait_send)
    for d in range(2):
        whole, rest = divmod(sum(hops(p, d) for p in range(PIECES)), PIECES)
        take(gat.at[pl.ds(0, whole)], ring_send.at[d])
        if rest:
            take(gat.at[0, pl.ds(0, rest)], ring_send.at[d])
    take(gat.at[pl.ds(0, chips)], share_send)
    pl.when(provider)(lambda: take(col.at[pl.ds(0, 2 * (chips - 1))], col_send.at[0]))
    for p in range(PIECES):
        mine, top, _ = column_rows(ahead[p % 2])
        wanted = mine & (top == p) if p < 2 else mine
        pl.when(wanted)(lambda p=p: take(col.at[0, pl.ds(0, 2)], col_send.at[1 + p]))


def fused_device(n, ncol, record, shot_fire_samples):
    rows, length = record.shape
    chips = n // 2
    shot_fire_samples = pltpu.with_memory_space_constraint(shot_fire_samples, pltpu.HBM)
    gram = pl.pallas_call(
        functools.partial(kernel, n, ncol),
        out_shape=jax.ShapeDtypeStruct((8 * ncol, rows), jnp.float32),
        in_specs=[
            pl.BlockSpec(memory_space=pltpu.HBM),
            pl.BlockSpec(memory_space=pltpu.HBM),
        ],
        out_specs=pl.BlockSpec(memory_space=pltpu.VMEM),
        scratch_shapes=[
            pltpu.SMEM(shot_fire_samples.shape, jnp.int32),
            pltpu.SemaphoreType.DMA,
            pltpu.VMEM((rows, length), jnp.bfloat16),
            pltpu.VMEM((8, LANES), jnp.int32),
            pltpu.VMEM((8, LANES), jnp.int32),
            pltpu.VMEM((2, SPACING, LANES), jnp.float32),
            pltpu.VMEM((2, 3 * GROUP, 16, LANES), jnp.bfloat16),
            pltpu.VMEM((2 * GROUP * SPACING, LANES), jnp.bfloat16),
            pltpu.VMEM((GROUP * SPACING, 2 * LANES), jnp.bfloat16),
            pltpu.VMEM((GROUP * SPACING, LANES), jnp.bfloat16),
            pltpu.VMEM((GROUP * SPACING, LANES), jnp.bfloat16),
            pltpu.VMEM((rows // 2, LANES), jnp.bfloat16),
            pltpu.VMEM((rows // 2, LANES), jnp.bfloat16),
            pltpu.VMEM((n, PIECES, rows // 2, LANES), jnp.bfloat16),
            pltpu.VMEM((n, 3, ncol, LANES), jnp.bfloat16),
            pltpu.VMEM((8 * ncol, 8 * LANES), jnp.bfloat16),
            pltpu.SemaphoreType.DMA((length // (GROUP * SPACING),)),
            pltpu.SemaphoreType.DMA((2,)),
            pltpu.SemaphoreType.DMA((2,)),
            pltpu.SemaphoreType.DMA((2,)),
            pltpu.SemaphoreType.DMA,
            pltpu.SemaphoreType.DMA((chips, PIECES)),
            pltpu.SemaphoreType.DMA((chips,)),
            pltpu.SemaphoreType.DMA((1 + PIECES,)),
            pltpu.SemaphoreType.DMA((n,)),
        ],
        compiler_params=pltpu.CompilerParams(
            collective_id=0, has_side_effects=True, vmem_limit_bytes=50 * 1024 * 1024
        ),
    )(shot_fire_samples, record)
    return gram.reshape(2, 4, ncol, rows).transpose(0, 1, 3, 2)


def whole_step(n, receivers, record, shot_fire_samples):
    rows, length = record.shape
    shots = shot_fire_samples.shape[0]
    ncol = receivers // n
    fits = (
        receivers == 2 * rows and ncol % 16 == 0 and rows % (4 * ncol) == 0
        and shots == 2 * HALF and length == shots * SPACING and n % 8 == 0
    )
    if fits:
        return fused_device(n, ncol, record, shot_fire_samples)
    return per_device(record, shot_fire_samples)


def solution(mesh):
    def step(record, shot_fire_samples):
        body = functools.partial(whole_step, mesh.shape["shot"], record.shape[0])
        return jax.shard_map(
            body,
            mesh=mesh,
            in_specs=(P("rcv", "shot"), P("shot")),
            out_specs=P(None, None, "rcv", "shot"),
            check_vma=False,
        )(record, shot_fire_samples)

    return step
```

```python
import functools
import math

import jax
import jax.numpy as jnp
from jax import lax
from jax.experimental import pallas as pl
from jax.experimental.pallas import tpu as pltpu
from jax.sharding import PartitionSpec as P

WIN = 2048
SPACING = 256


freq_bins = (24, 40, 56, 80)


def shifted(block, axis, distance):
    devices = range(lax.axis_size(axis))
    route = [(i - distance, i) for i in devices if i - distance in devices]
    return lax.ppermute(block, axis, route)


def dft_table(window_len):
    lag_index = jnp.arange(window_len, dtype=jnp.int32)
    bin_list = jnp.array(freq_bins, dtype=jnp.int32)
    turn_count = lag_index[:, None] * bin_list[None, :] % window_len
    phase_angle = 2.0 * math.pi / window_len * turn_count.astype(jnp.float32)
    dft_rows = jnp.concatenate([jnp.cos(phase_angle), -jnp.sin(phase_angle)], axis=1) / math.sqrt(
        window_len
    )
    return dft_rows.astype(jnp.bfloat16)


def shifted_tables(jitter, span):
    lag_index = jnp.arange(span, dtype=jnp.int32)[None, :] - jitter[:, None]
    inside = (lag_index >= 0) & (lag_index < WIN)
    clipped = jnp.clip(lag_index, 0, WIN - 1)
    bin_list = jnp.array(freq_bins, dtype=jnp.int32)
    turn_count = clipped[:, None, :] * bin_list[None, :, None] % WIN
    phase_angle = 2.0 * math.pi / WIN * turn_count.astype(jnp.float32)
    table = jnp.concatenate([jnp.cos(phase_angle), -jnp.sin(phase_angle)], axis=1) / math.sqrt(WIN)
    table = jnp.where(inside[:, None, :], table, 0.0)
    return table.astype(jnp.bfloat16)


def local_spectra(extended, sample_offsets, dft_rows):
    count_of_shots = sample_offsets.shape[0]
    reach_blocks = WIN // SPACING + 1
    jitter = sample_offsets - jnp.arange(count_of_shots, dtype=jnp.int32) * SPACING
    tables = shifted_tables(jitter, reach_blocks * SPACING)
    tables = tables.reshape(count_of_shots, dft_rows.shape[1], reach_blocks, SPACING)
    blocks = extended.reshape(extended.shape[0], extended.shape[1] // SPACING, SPACING)
    total = jnp.zeros((count_of_shots, dft_rows.shape[1], extended.shape[0]), jnp.float32)
    for offset in range(reach_blocks):
        record_part = blocks[:, offset : offset + count_of_shots, :]
        total = total + jnp.einsum(
            "rsu,scu->scr", record_part, tables[:, :, offset, :], preferred_element_type=jnp.float32
        )
    return total


def gram_terms(left, right):
    nfreq = len(freq_bins)
    left_re = left[:, :nfreq, :]
    left_im = left[:, nfreq:, :]
    right_re = right[:, :nfreq, :]
    right_im = right[:, nfreq:, :]
    gram_real = jnp.einsum("sfr,sfq->frq", left_re, right_re, preferred_element_type=jnp.float32)
    gram_real = gram_real + jnp.einsum(
        "sfr,sfq->frq", left_im, right_im, preferred_element_type=jnp.float32
    )
    gram_imag = jnp.einsum("sfr,sfq->frq", left_re, right_im, preferred_element_type=jnp.float32)
    gram_imag = gram_imag - jnp.einsum(
        "sfr,sfq->frq", left_im, right_re, preferred_element_type=jnp.float32
    )
    return jnp.stack([gram_real, gram_imag], axis=0)


def per_device(record, shot_fire_samples):
    trace_segment_length = record.shape[1]
    count_of_shots = shot_fire_samples.shape[0]
    dft_rows = dft_table(WIN)
    sample_offsets = shot_fire_samples - lax.axis_index("shot") * trace_segment_length
    head_rows = record[:, :WIN]
    rim_rows = shifted(head_rows, "shot", -1)
    extended = jnp.concatenate([record, rim_rows], axis=1)
    trace_spectra = local_spectra(extended, sample_offsets, dft_rows)
    trace_spectra = trace_spectra.astype(jnp.bfloat16)
    all_receivers = lax.all_gather(trace_spectra, "rcv", axis=2, tiled=True)
    total_shots = count_of_shots * lax.axis_size("shot")
    row_side = lax.all_gather(trace_spectra, "shot", axis=0, tiled=True)
    column_side = lax.all_to_all(all_receivers, "shot", split_axis=2, concat_axis=0, tiled=True)
    result = gram_terms(row_side, column_side)
    return result / total_shots


LANES = 128
HALF = 16
GROUP = 8
PIECES = 4
MESH = pl.DeviceIdType.MESH


def lane_fields(shape):
    lane = lax.broadcasted_iota(jnp.int32, shape, len(shape) - 1)
    return lane // 16 % 4, lane // 8 % 2, lane // 64 * 8 + lane % 8


def rotated(lag, quarter):
    freq, part, _ = lane_fields((1, LANES))
    bins = jnp.full((1, LANES), freq_bins[0], jnp.int32)
    for f in range(1, len(freq_bins)):
        bins = jnp.where(freq == f, freq_bins[f], bins)
    turn = (lag & (SPACING - 1)) * bins + (part * quarter[0] + quarter[1]) * (WIN // 4)
    turn = ((turn + WIN // 2) & (WIN - 1)) - WIN // 2
    x = (math.pi / WIN) * turn.astype(jnp.float32)
    y = x * x
    series = 1.0 / math.factorial(13)
    for k in (11, 9, 7, 5, 3, 1):
        series = series * y + (-1.0) ** (k // 2) / math.factorial(k)
    half_sine = x * series
    return 1.0 - 2.0 * half_sine * half_sine


EVENTS = (
    ('own', 0),
    ('arr', 1, 0, 1),
    ('arr', 1, 0, 0),
    ('own', 1),
    ('arr', 1, 2, 0),
    ('arr', 1, 1, 1),
    ('arr', 1, 1, 0),
    ('arr', 1, 3, 1),
    ('arr', 2, 0, 0),
    ('arr', 1, 2, 1),
    ('arr', 1, 3, 0),
    ('arr', 2, 0, 1),
    ('arr', 2, 1, 1),
    ('gram', ((0, 0, 1),)),
    ('arr', 2, 2, 0),
    ('arr', 2, 1, 0),
    ('gram', ((0, 0, 0),)),
    ('arr', 2, 3, 1),
    ('arr', 2, 3, 0),
    ('arr', 2, 2, 1),
    ('arr', 3, 0, 1),
    ('arr', 3, 0, 0),
    ('arr', 3, 1, 1),
    ('arr', 3, 2, 0),
    ('gram', ((2, 0, 0),)),
    ('arr', 3, 3, 1),
    ('gram', ((1, 0, 1), (1, 1, 0), (2, 0, 1), (2, 1, 0))),
    ('arr', 3, 2, 1),
    ('arr', 3, 1, 0),
    ('arr', 3, 3, 0),
    ('gram', ((1, 1, 1), (2, 1, 1), (1, 0, 0))),
    ('arr', 4, 0, 0),
    ('gram', ((3, 1, 0), (3, 1, 1))),
    ('arr', 4, 1, 1),
    ('arr', 4, 2, 0),
    ('arr', 4, 3, 1),
    ('gram', ((4, 0, 0), (3, 0, 0), (3, 0, 1))),
    ('gram', ((4, 0, 1),)),
)


def plain_events(half):
    def legs(t, p):
        return [("arr", t, p, d) for d in (p % 2, 1 - p % 2) if t <= (half if p % 2 == d else half - 1)]

    def sums(t):
        sides = (0,) if t in (0, half) else (0, 1)
        return tuple((t, d, other) for other in range(2) for d in sides)

    events = [("own", 0), *legs(1, 0), *legs(1, 1), ("own", 1), *legs(1, 2), ("gram", sums(0)), *legs(1, 3)]
    for t in range(2, half + 1):
        events += [*legs(t, 0), *legs(t, 1), *legs(t, 2), ("gram", sums(t - 1)), *legs(t, 3)]
    return [*events, *(("gram", (one,)) for one in sums(half))]


def kernel(
    n, ncol, fire_hbm, rec_ref, out_ref,
    fire_ref, fire_sem, rec, joff, poff, wave, mask, tm0, tmc, tm1, tmf, rim_out, rim_in, gat, col, rmat,
    rec_sem, jit_sem, rim_sem, ring_send, share_send, ring_recv, share_recv, col_send, col_recv,
):
    me = lax.axis_index("shot")
    mj = lax.axis_index("rcv")
    rows = rec.shape[0]
    fold = rows // 2
    span = GROUP * SPACING
    chips = n // 2
    nz = chips // 2
    half = chips // 2
    reach = WIN // SPACING
    core = me % 2
    chip = me // 2
    z, y = chip // 2, chip % 2
    pos = jnp.where(y == 0, z, chips - 1 - z)

    def chip_at(position):
        q = (position + 2 * chips) % chips
        second = q >= nz
        zz = jnp.where(second, chips - 1 - q, q)
        return zz * 2 + jnp.where(second, 1, 0)

    ahead = (chip_at(pos + 1), chip_at(pos - 1))
    pair = chip * 2 + (1 - core)
    has_prev, has_next = me > 0, me < n - 1
    prev, nxt = jnp.maximum(me - 1, 0), jnp.minimum(me + 1, n - 1)

    def load(g):
        part = pl.ds(g * span, span)
        return pltpu.make_async_copy(rec_ref.at[:, part], rec.at[:, part], rec_sem.at[g])

    fires = pltpu.make_async_copy(fire_hbm, fire_ref, fire_sem)
    fires.start()
    for g in range(3):
        load(g).start()

    barrier = pltpu.get_barrier_semaphore()

    def greet(other, column):
        pl.semaphore_signal(barrier, inc=1, device_id=(other, column), device_id_type=MESH)

    pl.when(has_prev)(lambda: greet(prev, mj))
    pl.when(has_next)(lambda: greet(nxt, mj))
    greet(pair, mj)
    for other in ahead:
        greet(other * 2 + core, mj)
    for which in range(2):
        greet(chip * 2 + which, 1 - mj)
    greeted = 5 + has_prev.astype(jnp.int32) + has_next.astype(jnp.int32)

    freq, part_of, shot_lane = lane_fields((1, LANES))
    lower_lanes = lax.broadcasted_iota(jnp.int32, (1, LANES), 1) < LANES // 2
    row_index = lax.broadcasted_iota(jnp.int32, (16, LANES), 0)
    fine = [rotated(row_index, (1, quarter)) * (1.0 / math.sqrt(WIN)) for quarter in (0, -1)]
    coarse = [rotated(row_index * 16, (0, quarter)) for quarter in (0, -1)]
    for c in range(SPACING // 16):
        at, (cosine, sine) = slice(c * 16, (c + 1) * 16), (turn[c : c + 1] for turn in coarse)
        wave[0, at] = fine[0] * cosine - fine[1] * sine
        wave[1, at] = fine[1] * cosine + fine[0] * sine
    for rel in range(3 * GROUP):
        order = rel - lane_fields((16, LANES))[2]
        early = (order >= 0) & (order < reach)
        late = (order >= 1) & (order <= reach)
        mask[0, rel] = early.astype(jnp.float32).astype(jnp.bfloat16)
        mask[1, rel] = late.astype(jnp.float32).astype(jnp.bfloat16)
    out_ref[...] = jnp.zeros_like(out_ref)
    fires.wait()
    jitters = []
    for h in range(2):
        row = jnp.zeros((1, LANES), jnp.int32)
        for s in range(HALF):
            row = jnp.where(shot_lane == s, fire_ref[h * HALF + s], row)
        jitters.append(row & (SPACING - 1))
    joff[...] = jnp.broadcast_to(jitters[1], joff.shape)

    @pl.when(me == 0)
    def _():
        poff[...] = jnp.zeros_like(poff)

    jitter = pltpu.make_async_remote_copy(
        joff, poff, jit_sem.at[0], jit_sem.at[1], device_id=(nxt, mj), device_id_type=MESH
    )
    rim = pltpu.make_async_remote_copy(
        rim_out, rim_in, rim_sem.at[0], rim_sem.at[1], device_id=(prev, mj), device_id_type=MESH
    )

    def fill(start, places):
        turned = rotated(start, (0, 0)), rotated(start, (0, -1))
        for c in range(SPACING // 16):
            part = slice(c * 16, (c + 1) * 16)
            value = wave[0, part] * turned[0] + wave[1, part] * turned[1]
            inside = lax.broadcasted_iota(jnp.int32, (16, LANES), 0) + c * 16 >= start
            early = jnp.where(inside, value, 0.0).astype(jnp.bfloat16)
            late = jnp.where(inside, 0.0, value).astype(jnp.bfloat16)
            for rel, (ref, block, lanes) in places.items():
                at = slice(block * SPACING + c * 16, block * SPACING + (c + 1) * 16)
                ref[at, lanes] = early * mask[0, rel] + late * mask[1, rel]

    low, high = slice(0, LANES), slice(LANES, 2 * LANES)

    def two_dots(block, count, ref, first):
        parts = []
        for k in range(2):
            b, f = block + k * count, first + k * count
            parts.append(
                jnp.dot(
                    rec[:, b * SPACING : (b + count) * SPACING],
                    ref[f * SPACING : (f + count) * SPACING, :],
                    preferred_element_type=jnp.float32,
                )
            )
        return parts[0] + parts[1]

    def folded(value, second):
        top, bottom = value[:fold], value[fold:]
        if second:
            return jnp.where(lower_lanes, pltpu.roll(top, LANES // 2, 1), bottom)
        return jnp.where(lower_lanes, top, pltpu.roll(bottom, LANES // 2, 1))

    def ring(src, p, d):
        return pltpu.make_async_remote_copy(
            gat.at[src, p], gat.at[src, p], ring_send.at[d], ring_recv.at[src // 2, p],
            device_id=(ahead[d] * 2 + core, mj), device_id_type=MESH,
        )

    def share(src, p):
        return pltpu.make_async_remote_copy(
            gat.at[src, p], gat.at[src, p], share_send, share_recv.at[src // 2],
            device_id=(pair, mj), device_id_type=MESH,
        )

    def column_rows(target):
        home = target * 2 * ncol // rows
        first = target * 2 * ncol - home * rows
        top = first // fold
        return home == mj, top, pl.multiple_of(first - top * fold, 16)

    def send_col(src, p, target, sem):
        mine, top, first = column_rows(target)
        wanted = mine & (top == p) if p < 2 else mine

        @pl.when(wanted)
        def _():
            for which in range(2):
                pltpu.make_async_remote_copy(
                    gat.at[src, p, pl.ds(first + which * ncol, ncol), :], col.at[src, max(p - 1, 0)],
                    col_send.at[sem], col_recv.at[src],
                    device_id=(target * 2 + which, 1 - mj), device_id_type=MESH,
                ).start()

    def hops(p, d):
        return half if p % 2 == d else half - 1

    def source(t, d, which):
        return chip_at(pos - t if d == 0 else pos + t) * 2 + which

    def send_own(p):
        for d in (p % 2, 1 - p % 2):
            ring(me, p, d).start()

    def spread(src, p):
        share(src, p).start()
        send_col(src, p, chip, 0)

    def arrive(t, p, d):
        src = source(t, d, core)
        ring(src, p, d).wait_recv()
        if t < hops(p, d):
            ring(src, p, d).start()
        if t == half - 1 and hops(p, d) == half:
            send_col(src, p, ahead[d], 1 + p)
        if t < half:
            spread(src, p)
        else:
            share(src, p).start()

    provider, col_top, col_first = column_rows(chip)
    own_first = pl.multiple_of(col_first + core * ncol, 16)

    def take(buffer, sem):
        pltpu.make_async_copy(buffer, buffer, sem).wait()

    def gram(sources, last=False):
        for src, shared in sources:
            if shared:
                take(gat.at[src], share_recv.at[src // 2])

        @pl.when(provider)
        def _():
            for src, _ in sources:
                for k, p in enumerate((col_top, 2, 3)):
                    col[src, k] = gat[src, p, pl.ds(own_first, ncol), :]

        @pl.when(jnp.logical_not(provider))
        def _():
            for src, _ in sources:
                take(col.at[src], col_recv.at[src])

        lefts = []
        for slot, (src, _) in enumerate(sources):
            xa, xb, xc = (col[src, k].astype(jnp.float32) for k in range(3))
            top = col_top == 0
            xb = jnp.where(top, xb, pltpu.roll(xb, LANES // 2, 1))
            xc = jnp.where(top, pltpu.roll(xc, LANES // 2, 1), xc)
            for h, x in enumerate((xa, jnp.where(lower_lanes, xb, xc))):
                at = slice((2 * slot + h) * LANES, (2 * slot + h + 1) * LANES)
                swapped = jnp.where(part_of == 0, pltpu.roll(x, LANES - 8, 1), -pltpu.roll(x, 8, 1))
                for ri, value in enumerate((x, swapped)):
                    for f in range(4):
                        rmat[pl.ds((ri * 4 + f) * ncol, ncol), at] = jnp.where(
                            freq == f, value, 0.0
                        ).astype(jnp.bfloat16)
            b, c = gat[src, 2], gat[src, 3]
            k = LANES // 2
            lefts.append(
                jnp.concatenate(
                    [
                        jnp.concatenate([gat[src, 0], b[:, :k], c[:, :k]], axis=1),
                        jnp.concatenate([gat[src, 1], b[:, k:], c[:, k:]], axis=1),
                    ],
                    axis=0,
                )
            )
        total = out_ref[...] + lax.dot_general(
            rmat[:, : 2 * LANES * len(sources)], jnp.concatenate(lefts, axis=1),
            (((1,), (1,)), ((), ())), preferred_element_type=jnp.float32,
        )
        out_ref[...] = total * (1.0 / (n * 2 * HALF)) if last else total

    def grams(t):
        found = []
        for other in range(2):
            for d in range(2):
                if d == 1 and t in (0, half):
                    continue
                found.append((source(t, d, 1 - core if other else core), other == 1))
        return found

    fill(jitters[0], {r: (tm0, r, low) for r in range(16)})
    fill(jitters[0], {16 + r: (tmc, r, low) for r in range(8)})
    fill(jitters[1], {r: (tmc, r, high) for r in range(8)})
    load(3).start()
    pl.semaphore_wait(barrier, greeted)
    pl.when(has_next)(jitter.start)
    load(0).wait()
    first_half = two_dots(0, 4, tm0, 0)
    for g in (1, 2):
        load(g).wait()
    first_half = first_half + two_dots(8, 4, tm0, 8)
    middle = two_dots(16, 4, tmc, 0)
    first_half = (first_half + middle[:, :LANES]).astype(jnp.bfloat16)
    for p in range(2):
        gat[me, p] = first_half[p * fold : (p + 1) * fold]
    for p in range(2):
        send_own(p)
    load(3).wait()
    fill(jitters[1], {8 + r: (tm1, r, low) for r in range(8)})
    second_half = middle[:, LANES:] + two_dots(24, 4, tm1, 0)
    gat[me, 2] = folded(second_half, False).astype(jnp.bfloat16)
    pl.when(has_prev)(jitter.wait_recv)
    fill(poff[0:1, :], {16 + r: (tmf, r, low) for r in range(8)})
    rim_out[...] = folded(out_ref[:, :LANES] + two_dots(0, 4, tmf, 0), True).astype(jnp.bfloat16)
    pl.when(has_prev)(rim.start)
    send_own(2)
    for p in range(3):
        spread(me, p)
    edge = folded(second_half, True)

    def finish():
        pl.when(has_next)(rim.wait_recv)
        outer = jnp.where(has_next, rim_in[...].astype(jnp.float32), 0.0)
        gat[me, 3] = (edge + outer).astype(jnp.bfloat16)
        send_own(3)
        spread(me, 3)

    def arrivals(t, p):
        for d in (p % 2, 1 - p % 2):
            if t <= hops(p, d):
                arrive(t, p, d)

    events = EVENTS if half == 4 else plain_events(half)
    for event in events:
        if event[0] == "own":
            pl.when(core == event[1])(finish)
        elif event[0] == "arr":
            arrive(*event[1:])
        else:
            group = [(source(t, d, 1 - core if other else core), other == 1) for t, d, other in event[1]]
            gram(group, last=event is events[-1])

    pl.when(has_next)(jitter.wait_send)
    pl.when(has_prev)(rim.wait_send)
    for d in range(2):
        whole, rest = divmod(sum(hops(p, d) for p in range(PIECES)), PIECES)
        take(gat.at[pl.ds(0, whole)], ring_send.at[d])
        if rest:
            take(gat.at[0, pl.ds(0, rest)], ring_send.at[d])
    take(gat.at[pl.ds(0, chips)], share_send)
    pl.when(provider)(lambda: take(col.at[pl.ds(0, 2 * (chips - 1))], col_send.at[0]))
    for p in range(PIECES):
        mine, top, _ = column_rows(ahead[p % 2])
        wanted = mine & (top == p) if p < 2 else mine
        pl.when(wanted)(lambda p=p: take(col.at[0, pl.ds(0, 2)], col_send.at[1 + p]))


def fused_device(n, ncol, record, shot_fire_samples):
    rows, length = record.shape
    chips = n // 2
    shot_fire_samples = pltpu.with_memory_space_constraint(shot_fire_samples, pltpu.HBM)
    gram = pl.pallas_call(
        functools.partial(kernel, n, ncol),
        out_shape=jax.ShapeDtypeStruct((8 * ncol, rows), jnp.float32),
        in_specs=[
            pl.BlockSpec(memory_space=pltpu.HBM),
            pl.BlockSpec(memory_space=pltpu.HBM),
        ],
        out_specs=pl.BlockSpec(memory_space=pltpu.VMEM),
        scratch_shapes=[
            pltpu.SMEM(shot_fire_samples.shape, jnp.int32),
            pltpu.SemaphoreType.DMA,
            pltpu.VMEM((rows, length), jnp.bfloat16),
            pltpu.VMEM((8, LANES), jnp.int32),
            pltpu.VMEM((8, LANES), jnp.int32),
            pltpu.VMEM((2, SPACING, LANES), jnp.float32),
            pltpu.VMEM((2, 3 * GROUP, 16, LANES), jnp.bfloat16),
            pltpu.VMEM((2 * GROUP * SPACING, LANES), jnp.bfloat16),
            pltpu.VMEM((GROUP * SPACING, 2 * LANES), jnp.bfloat16),
            pltpu.VMEM((GROUP * SPACING, LANES), jnp.bfloat16),
            pltpu.VMEM((GROUP * SPACING, LANES), jnp.bfloat16),
            pltpu.VMEM((rows // 2, LANES), jnp.bfloat16),
            pltpu.VMEM((rows // 2, LANES), jnp.bfloat16),
            pltpu.VMEM((n, PIECES, rows // 2, LANES), jnp.bfloat16),
            pltpu.VMEM((n, 3, ncol, LANES), jnp.bfloat16),
            pltpu.VMEM((8 * ncol, 8 * LANES), jnp.bfloat16),
            pltpu.SemaphoreType.DMA((length // (GROUP * SPACING),)),
            pltpu.SemaphoreType.DMA((2,)),
            pltpu.SemaphoreType.DMA((2,)),
            pltpu.SemaphoreType.DMA((2,)),
            pltpu.SemaphoreType.DMA,
            pltpu.SemaphoreType.DMA((chips, PIECES)),
            pltpu.SemaphoreType.DMA((chips,)),
            pltpu.SemaphoreType.DMA((1 + PIECES,)),
            pltpu.SemaphoreType.DMA((n,)),
        ],
        compiler_params=pltpu.CompilerParams(
            collective_id=0, has_side_effects=True, vmem_limit_bytes=50 * 1024 * 1024
        ),
    )(shot_fire_samples, record)
    return gram.reshape(2, 4, ncol, rows).transpose(0, 1, 3, 2)


def whole_step(n, receivers, record, shot_fire_samples):
    rows, length = record.shape
    shots = shot_fire_samples.shape[0]
    ncol = receivers // n
    fits = (
        receivers == 2 * rows and ncol % 16 == 0 and rows % (4 * ncol) == 0
        and shots == 2 * HALF and length == shots * SPACING and n % 8 == 0
    )
    if fits:
        return fused_device(n, ncol, record, shot_fire_samples)
    return per_device(record, shot_fire_samples)


def solution(mesh):
    def step(record, shot_fire_samples):
        body = functools.partial(whole_step, mesh.shape["shot"], record.shape[0])
        return jax.shard_map(
            body,
            mesh=mesh,
            in_specs=(P("rcv", "shot"), P("shot")),
            out_specs=P(None, None, "rcv", "shot"),
            check_vma=False,
        )(record, shot_fire_samples)

    return step
```
